32 devices in a mesh: pages: 16 (over z, x, core), tok: 2 (over y).
Axes of the slice: x: 2, y: 2, z: 4, core: 2. Of those that a mesh axis runs over, the one named last changes fastest.
Arguments:
- queries: bfloat16 [32, 32, 128], P('pages'), may hold values from -50 to 50
- pages: bfloat16 [16, 1024, 128], P('pages', 'tok'), may hold values from -10 to 10
- pad_counts: int32 [16], P('pages'), may hold values from 0 to 511
- labels: int32 [32, 16], P(None, 'pages'), may hold values 0 or 1
Outputs:
- query_grad: float32 [32, 32, 128], P('pages')
- page_grad: float32 [16, 1024, 128], P('pages', 'tok')
- page_loss: float32 [16], P('pages')
The draws below stay inside these ranges and needn't reach their ends.
All inputs are finite; a program needn't handle non-finite values. No bound on the sum of `labels` on one device may be relied on, other than what follows from the above.
Results may differ from the reference program's by a relative error of at most 0.0025.
Values may be sent and summed in bfloat16 or wider, within the bound.
No kernel may reach another device: no remote copies, remote signals or barrier semaphores. Data moves between devices by JAX's collectives and lax.ppermute only.
A program may use at most 64 MiB of HBM per device.

```python
import math
import jax
import jax.numpy as jnp
from jax import lax

E = 128
LQ = 32
LP = 1024
NQ = 32
NP = 16


def shared_tables(key):
    page_key = jax.random.fold_in(key, 7101)
    query_key = jax.random.fold_in(key, 7102)
    pages = jnp.clip(jax.random.normal(page_key, (NP, LP, E), jnp.float32), -6.0, 6.0)
    queries = jnp.clip(jax.random.normal(query_key, (NQ, LQ, E), jnp.float32), -6.0, 6.0)
    return (pages, queries)


def draw_queries(key, part):
    return shared_tables(key)[1].astype(jnp.bfloat16)


def draw_pages(key, part):
    return shared_tables(key)[0].astype(jnp.bfloat16)


def touch_ends(entries, stream_key, smallest, largest):
    place = [jax.random.randint(jax.random.fold_in(stream_key, axis), (), 0, length) for axis, length in enumerate(entries.shape)]
    main_axis = entries.shape.index(max(entries.shape))
    beside = place[:main_axis] + [(place[main_axis] + 1) % entries.shape[main_axis]] + place[main_axis + 1:]
    return entries.at[tuple(place)].set(smallest).at[tuple(beside)].set(largest)


def setup_inputs(seed: int = 0) -> dict:
    key_of = jax.random.split(jax.random.key(seed), 5)
    queries = draw_queries(jax.random.fold_in(key_of[4], 71), 0)
    pages = draw_pages(jax.random.fold_in(key_of[4], 71), 0)
    pad_counts = touch_ends(jax.random.randint(key_of[2], (NP,), 0, LP // 2), jax.random.fold_in(key_of[2], 1), 0, (LP // 2) - 1).astype(jnp.int32)
    labels = touch_ends((jax.random.randint(key_of[3], (NQ, NP), 0, 16) < 1).astype(jnp.int32), jax.random.fold_in(key_of[3], 1), 0, 1)
    return dict(queries=queries, pages=pages, pad_counts=pad_counts, labels=labels)


MASKED = -1.0e9
LOGIT_SPAN = 8.0
CENTRE_SHIFT = 0.5
FILL_SHARE = 0.75


def page_scores(query_rows, page_rows, usable):
    raw = jnp.dot(query_rows, page_rows.T, preferred_element_type=jnp.float32) * (E ** -0.5)
    return jnp.where(usable[None, :], raw, MASKED)


def smooth_max(scores):
    highest = jnp.max(scores, axis=1)
    return highest + jnp.log(jnp.sum(jnp.exp(scores - highest[:, None]), axis=1))


def reference(queries, pages, pad_counts, labels):
    query_rows = queries.reshape(NQ * LQ, E)
    positions = jnp.arange(LP, dtype=jnp.int32)
    usable = positions[None, :] < (LP - pad_counts)[:, None]

    def forward_page(packed):
        page_rows, page_usable = packed
        return smooth_max(page_scores(query_rows, page_rows, page_usable))

    smooth = lax.map(forward_page, (pages, usable))
    similarity = smooth.reshape(NP, NQ, LQ).sum(axis=2).T
    label_sign = 2.0 * labels.astype(jnp.float32) - 1.0
    logit_gain = LOGIT_SPAN / LQ
    centre = LQ * (CENTRE_SHIFT + math.log(FILL_SHARE * LP))
    logits = logit_gain * (similarity - centre)
    page_loss = jnp.sum(jax.nn.softplus(-label_sign * logits), axis=0)
    slope = logit_gain * (-label_sign * jax.nn.sigmoid(-label_sign * logits))
    row_slope = jnp.repeat(slope.T, LQ, axis=1)

    def backward_page(running, packed):
        page_rows, page_usable, page_smooth, page_slope = packed
        scores = page_scores(query_rows, page_rows, page_usable)
        weights = jnp.where(page_usable[None, :], jnp.exp(scores - page_smooth[:, None]), 0.0)
        scaled = (weights * page_slope[:, None]).astype(jnp.bfloat16)
        running = running + jnp.dot(scaled, page_rows, preferred_element_type=jnp.float32) * (E ** -0.5)
        page_term = jnp.dot(scaled.T, query_rows, preferred_element_type=jnp.float32) * (E ** -0.5)
        return running, page_term

    query_sum, page_grad = lax.scan(backward_page, jnp.zeros((NQ * LQ, E), jnp.float32), (pages, usable, smooth, row_slope))
    return query_sum.reshape(NQ, LQ, E), page_grad, page_loss
```

```python
import functools
import math

import jax
import jax.numpy as jnp
from jax import lax
from jax.experimental import pallas as pl
from jax.experimental.pallas import tpu as pltpu
from jax.sharding import PartitionSpec as P

MASKED = -1.0e30
LOGIT_SPAN = 8.0
CENTRE_SHIFT = 0.5
FILL_SHARE = 0.75
LANES = 128
ROW_BLOCK = 512
VMEM_BYTES = 24 * 2**20


def over_tokens(left, right):
    return lax.dot_general(left, right, (((0,), (0,)), ((), ())), preferred_element_type=jnp.float32)


def over_features(left, right):
    return lax.dot_general(left, right, (((1,), (1,)), ((), ())), preferred_element_type=jnp.float32)


def group_sums(values, width):
    lane = lax.broadcasted_iota(jnp.int32, values.shape, 1)
    step = 1
    while step < width:
        below = pltpu.roll(values, step, 1)
        above = pltpu.roll(values, LANES - step, 1)
        values = values + jnp.where((lane & step) != 0, below, above)
        step *= 2
    return values


def body(
    query_len, page_len, copies, limits_ref, rows_ref, mine_ref, other_ref, sign_ref,
    blocks_ref, own_ref, sent_ref, loss_ref, own_sum, other_sum,
):
    row_count, width = rows_ref.shape
    tokens = mine_ref.shape[0]
    scale = width ** (-0.5)
    rate = scale * math.log2(math.e)
    gain = LOGIT_SPAN / query_len
    centre = query_len * (CENTRE_SHIFT + math.log(FILL_SHARE * page_len))
    block_rows = math.gcd(row_count, ROW_BLOCK)
    block_count = row_count // block_rows
    pieces = block_rows // LANES
    mine = mine_ref[...]
    other = other_ref[...]

    def one_block(offset):
        query_rows = rows_ref[pl.ds(offset, block_rows), :]
        place = lax.broadcasted_iota(jnp.int32, (tokens, block_rows), 0)
        raw_own = jnp.where(place < limits_ref[0], over_features(mine, query_rows), MASKED)
        raw_other = jnp.where(place < limits_ref[1], over_features(other, query_rows), MASKED)
        highest = jnp.maximum(
            jnp.max(raw_own, axis=0, keepdims=True), jnp.max(raw_other, axis=0, keepdims=True)
        )
        exp_own = jnp.exp2((raw_own - highest) * rate)
        exp_other = jnp.exp2((raw_other - highest) * rate)
        total = jnp.sum(exp_own, axis=0, keepdims=True) + jnp.sum(exp_other, axis=0, keepdims=True)

        def stacked(v):
            return jnp.concatenate([v[:, LANES * k : LANES * (k + 1)] for k in range(pieces)], axis=0)

        sums = stacked(total)
        smooth = stacked(highest) * scale + jnp.log(sums)
        similarity = group_sums(smooth, query_len)
        sign = stacked(sign_ref[:, pl.ds(offset, block_rows)])
        against = -sign * (gain * (similarity - centre))
        small = jnp.exp(-jnp.abs(against))
        losses = jnp.maximum(against, 0.0) + jnp.log1p(small)
        sigmoid = jnp.where(against >= 0.0, 1.0, small) / (1.0 + small)
        factor = (-gain * sign) * sigmoid / sums
        factor = jnp.concatenate([factor[k : k + 1, :] for k in range(pieces)], axis=1)
        scaled_own = (exp_own * factor).astype(jnp.bfloat16)
        scaled_other = (exp_other * factor).astype(jnp.bfloat16)
        query_terms = over_tokens(mine, scaled_own) + over_tokens(other, scaled_other)
        query_terms = query_terms.T.astype(jnp.bfloat16)
        own_terms = jnp.dot(scaled_own, query_rows, preferred_element_type=jnp.float32)
        other_terms = jnp.dot(scaled_other, query_rows, preferred_element_type=jnp.float32)
        lane = lax.broadcasted_iota(jnp.int32, losses.shape, 1)
        loss = jnp.sum(jnp.where(lane % query_len == 0, losses, 0.0))
        return query_terms, own_terms, other_terms, loss

    dest_rows = blocks_ref.shape[2]
    dests = block_rows // dest_rows

    def put(index, query_terms):
        shaped = query_terms.reshape(dests, dest_rows, width)
        for k in range(copies):
            blocks_ref[pl.ds(index * dests, dests), k] = shaped

    if block_count == 1:
        query_terms, own_terms, other_terms, loss = one_block(0)
        put(0, query_terms)
    else:
        own_sum[...] = jnp.zeros_like(own_sum)
        other_sum[...] = jnp.zeros_like(other_sum)

        def step(index, loss_so_far):
            query_terms, own_terms, other_terms, loss = one_block(pl.multiple_of(index * block_rows, block_rows))
            put(index, query_terms)
            own_sum[...] += own_terms
            other_sum[...] += other_terms
            return loss_so_far + loss

        loss = lax.fori_loop(0, block_count, step, jnp.float32(0.0))
        own_terms = own_sum[...]
        other_terms = other_sum[...]
    own_ref[...] = own_terms * scale
    sent_ref[pl.ds(0, tokens), :] = (other_terms * scale).astype(jnp.bfloat16)
    loss_all = jnp.full(loss_ref.shape, loss, jnp.float32)
    loss_ref[...] = loss_all
    tail = sent_ref.shape[0] - tokens
    whole = jnp.full((tail, width), loss, jnp.float32)
    high = whole.astype(jnp.bfloat16)
    rest = whole - high.astype(jnp.float32)
    middle = rest.astype(jnp.bfloat16)
    low = (rest - middle.astype(jnp.float32)).astype(jnp.bfloat16)
    lane = lax.broadcasted_iota(jnp.int32, (tail, width), 1)
    parts = jnp.where(
        lane == 0,
        high.astype(jnp.float32),
        jnp.where(lane == 1, middle.astype(jnp.float32), low.astype(jnp.float32)),
    )
    sent_ref[pl.ds(tokens, tail), :] = parts.astype(jnp.bfloat16)


def on_device(queries, pages, pad_counts, labels):
    query_count, query_len, width = queries.shape
    _, tokens, _ = pages.shape
    owners = lax.axis_size("pages")
    shares = lax.axis_size("tok")
    if shares != 2 or query_count % shares:
        raise ValueError("unsupported split")
    share = lax.axis_index("tok")
    page_len = tokens * shares
    picked = query_count // shares
    dest_rows = picked * query_len
    swap = [(0, 1), (1, 0)]

    mine = pages[0]
    other = lax.ppermute(mine, "tok", swap)
    chosen = lax.dynamic_slice_in_dim(queries, share * picked, picked, 0).reshape(1, dest_rows, width)
    gathered = lax.all_to_all(
        jnp.broadcast_to(chosen, (owners, dest_rows, width)), "pages", 0, 0, tiled=True
    )
    rows = gathered.reshape(owners * dest_rows, width)
    usable = page_len - pad_counts[0]
    limits = jnp.stack([usable - share * tokens, usable - (1 - share) * tokens])
    label = lax.dynamic_slice_in_dim(labels.reshape(owners, query_count), share * picked, picked, 1)
    sign = jnp.repeat(2.0 * label.reshape(owners * picked).astype(jnp.float32) - 1.0, query_len)[None, :]

    row_count = owners * dest_rows
    tail = 16
    vmem = pl.BlockSpec(memory_space=pltpu.VMEM)
    blocks, own, sent, loss = pl.pallas_call(
        functools.partial(body, query_len, page_len, shares),
        out_shape=(
            jax.ShapeDtypeStruct((owners, shares, dest_rows, width), jnp.bfloat16),
            jax.ShapeDtypeStruct((tokens, width), jnp.float32),
            jax.ShapeDtypeStruct((tokens + tail, width), jnp.bfloat16),
            jax.ShapeDtypeStruct((8, LANES), jnp.float32),
        ),
        in_specs=[pl.BlockSpec(memory_space=pltpu.SMEM), vmem, vmem, vmem, vmem],
        out_specs=(vmem, vmem, vmem, vmem),
        scratch_shapes=[pltpu.VMEM((tokens, width), jnp.float32)] * 2,
        cost_estimate=pl.CostEstimate(
            flops=6 * row_count * page_len * width,
            transcendentals=row_count * page_len,
            bytes_accessed=4 * row_count * width + 10 * tokens * width,
        ),
        compiler_params=pltpu.CompilerParams(vmem_limit_bytes=VMEM_BYTES),
        name="page_step",
    )(limits, rows, mine, other, sign)

    partials = lax.all_to_all(
        blocks.reshape(owners * shares, dest_rows, width), ("pages", "tok"), 0, 0, tiled=True
    )
    received = lax.ppermute(sent, "tok", swap)
    page_grad = (own + received[:tokens].astype(jnp.float32))[None]
    extra = received[tokens, :3].astype(jnp.float32)
    page_loss = loss[0, :1] + (extra[0] + extra[1] + extra[2])
    summed = jnp.sum(
        partials.reshape(owners, shares, dest_rows, width).astype(jnp.float32), axis=0
    ) * (width ** (-0.5))
    query_grad = summed.reshape(query_count, query_len, width)
    return query_grad, page_grad, page_loss


def solution(mesh):
    return jax.shard_map(
        on_device,
        mesh=mesh,
        in_specs=(P("pages", None, None), P("pages", "tok", None), P("pages"), P(None, "pages")),
        out_specs=(P("pages", None, None), P("pages", "tok", None), P("pages")),
        check_vma=False,
    )
```

```python
import functools
import math

import jax
import jax.numpy as jnp
from jax import lax
from jax.experimental import pallas as pl
from jax.experimental.pallas import tpu as pltpu
from jax.sharding import PartitionSpec as P


MASKED = -1.0e30
LOGIT_SPAN = 8.0
CENTRE_SHIFT = 0.5
FILL_SHARE = 0.75
LANES = 128
ROW_BLOCK = 256
TAIL = 16
VMEM_BYTES = 24 * 2**20


def over_tokens(left, right):
    return lax.dot_general(left, right, (((0,), (0,)), ((), ())), preferred_element_type=jnp.float32)


def over_features(left, right):
    return lax.dot_general(left, right, (((1,), (1,)), ((), ())), preferred_element_type=jnp.float32)


def group_sums(values, width):
    lane = lax.broadcasted_iota(jnp.int32, values.shape, 1)
    step = 1
    while step < width:
        below = pltpu.roll(values, step, 1)
        above = pltpu.roll(values, LANES - step, 1)
        values = values + jnp.where((lane & step) != 0, below, above)
        step *= 2
    return values


def loss_parts(loss):
    whole = jnp.full((TAIL, LANES), loss, jnp.float32)
    high = whole.astype(jnp.bfloat16).astype(jnp.float32)
    middle = (whole - high).astype(jnp.bfloat16).astype(jnp.float32)
    low = whole - high - middle
    lane = lax.broadcasted_iota(jnp.int32, (TAIL, LANES), 1)
    parts = jnp.where(lane == 0, high, jnp.where(lane == 1, middle, jnp.where(lane == 2, low, 0.0)))
    return parts.astype(jnp.bfloat16)


def loss_of(parts):
    return jnp.sum(parts.astype(jnp.float32)[:1])


def step_body(
    query_len, page_len, copies, limits_ref, rows_ref, near_ref, far_ref, near2_ref, far2_ref, sign_ref,
    blocks_ref, near_out, far_out, sent_ref, loss_ref, *sums,
):
    row_count, width = rows_ref.shape
    tokens = near_ref.shape[0]
    scale = width ** (-0.5)
    rate = scale * math.log2(math.e)
    gain = LOGIT_SPAN / query_len
    centre = query_len * (CENTRE_SHIFT + math.log(FILL_SHARE * page_len))
    block_rows = math.gcd(row_count, ROW_BLOCK)
    block_count = row_count // block_rows
    pieces = block_rows // LANES

    def one_page(page, query_rows, near, far, offset):
        place = lax.broadcasted_iota(jnp.int32, (tokens, block_rows), 0)
        raw_near = jnp.where(place < limits_ref[2 * page], over_features(near, query_rows), MASKED)
        raw_far = jnp.where(place < limits_ref[2 * page + 1], over_features(far, query_rows), MASKED)
        highest = jnp.maximum(
            jnp.max(raw_near, axis=0, keepdims=True), jnp.max(raw_far, axis=0, keepdims=True)
        )
        exp_near = jnp.exp2((raw_near - highest) * rate)
        exp_far = jnp.exp2((raw_far - highest) * rate)
        total = jnp.sum(exp_near, axis=0, keepdims=True) + jnp.sum(exp_far, axis=0, keepdims=True)

        def stacked(v):
            return jnp.concatenate([v[:, LANES * k : LANES * (k + 1)] for k in range(pieces)], axis=0)

        sums = stacked(total)
        smooth = stacked(highest) * scale + jnp.log(sums)
        similarity = group_sums(smooth, query_len)
        sign = stacked(sign_ref[page : page + 1, pl.ds(offset, block_rows)])
        against = -sign * (gain * (similarity - centre))
        small = jnp.exp(-jnp.abs(against))
        losses = jnp.maximum(against, 0.0) + jnp.log1p(small)
        sigmoid = jnp.where(against >= 0.0, 1.0, small) / (1.0 + small)
        factor = (-gain * sign) * sigmoid / sums
        factor = jnp.concatenate([factor[k : k + 1, :] for k in range(pieces)], axis=1)
        scaled_near = (exp_near * factor).astype(jnp.bfloat16)
        scaled_far = (exp_far * factor).astype(jnp.bfloat16)
        query_terms = over_tokens(near, scaled_near) + over_tokens(far, scaled_far)
        near_terms = jnp.dot(scaled_near, query_rows, preferred_element_type=jnp.float32)
        far_terms = jnp.dot(scaled_far, query_rows, preferred_element_type=jnp.float32)
        lane = lax.broadcasted_iota(jnp.int32, losses.shape, 1)
        loss = jnp.sum(jnp.where(lane % query_len == 0, losses, 0.0))
        return query_terms, near_terms, far_terms, loss

    def one_block(offset):
        query_rows = rows_ref[pl.ds(offset, block_rows), :]
        terms, *first = one_page(0, query_rows, near_ref[...], far_ref[...], offset)
        terms2, *second = one_page(1, query_rows, near2_ref[...], far2_ref[...], offset)
        return (terms + terms2).T.astype(jnp.bfloat16), first, second

    dest_rows = blocks_ref.shape[2]
    dests = block_rows // dest_rows

    def put(index, query_terms):
        shaped = query_terms.reshape(dests, dest_rows, width)
        for k in range(copies):
            blocks_ref[pl.ds(index * dests, dests), k] = shaped

    if block_count == 1:
        query_terms, (near_sum, far_sum, loss), (near2_sum, far2_sum, loss2) = one_block(0)
        put(0, query_terms)
    else:
        for ref in sums:
            ref[...] = jnp.zeros_like(ref)

        def step(index, so_far):
            query_terms, first, second = one_block(pl.multiple_of(index * block_rows, block_rows))
            put(index, query_terms)
            for ref, value in zip(sums, (first[0], first[1], second[0], second[1])):
                ref[...] += value
            return so_far[0] + first[2], so_far[1] + second[2]

        loss, loss2 = lax.fori_loop(0, block_count, step, (jnp.float32(0.0), jnp.float32(0.0)))
        near_sum, far_sum, near2_sum, far2_sum = (ref[...] for ref in sums)
    near_out[...] = near_sum * scale
    far_out[...] = far_sum * scale
    sent_ref[pl.ds(0, tokens), :] = (near2_sum * scale).astype(jnp.bfloat16)
    sent_ref[pl.ds(tokens, tokens), :] = (far2_sum * scale).astype(jnp.bfloat16)
    sent_ref[pl.ds(2 * tokens, TAIL), :] = loss_parts(loss2)
    loss_ref[...] = jnp.full(loss_ref.shape, loss, jnp.float32)


def merge_body(far_ref, loss_ref, got_ref, sent_ref):
    tokens = far_ref.shape[0]
    total = far_ref[...] + got_ref[pl.ds(tokens, tokens), :].astype(jnp.float32)
    sent_ref[pl.ds(0, tokens), :] = total.astype(jnp.bfloat16)
    loss = jnp.max(loss_ref[...]) + loss_of(got_ref[pl.ds(2 * tokens, TAIL), :])
    sent_ref[pl.ds(tokens, TAIL), :] = loss_parts(loss)


def last_body(near_ref, loss_ref, got_ref, got2_ref, grad_ref, total_ref):
    tokens = near_ref.shape[0]
    grad_ref[0] = (
        near_ref[...]
        + got_ref[pl.ds(0, tokens), :].astype(jnp.float32)
        + got2_ref[pl.ds(0, tokens), :].astype(jnp.float32)
    )
    total_ref[0] = (
        jnp.max(loss_ref[...])
        + loss_of(got_ref[pl.ds(2 * tokens, TAIL), :])
        + loss_of(got2_ref[pl.ds(tokens, TAIL), :])
    )


def device_step(queries, pages, pad_counts, labels):
    query_count, query_len, width = queries.shape
    _, tokens, _ = pages.shape
    owners = lax.axis_size("pages")
    shares = lax.axis_size("tok")
    if shares != 2 or query_count % shares or owners % 2:
        raise ValueError("unsupported split")
    share = lax.axis_index("tok")
    side = lax.axis_index("pages") % 2
    page_len = tokens * shares
    picked = query_count // shares
    dest_rows = picked * query_len
    chips = owners // 2
    swap = [(0, 1), (1, 0)]
    partner = [(i, i ^ 1) for i in range(owners)]
    same_side = [[2 * j + c for j in range(chips)] for c in range(2)]
    same_side_all = [
        [(2 * j + c) * shares + k for j in range(chips) for k in range(shares)] for c in range(2)
    ]
    vmem = pl.BlockSpec(memory_space=pltpu.VMEM)
    smem = pl.BlockSpec(memory_space=pltpu.SMEM)
    params = pltpu.CompilerParams(vmem_limit_bytes=VMEM_BYTES)

    chosen = lax.dynamic_slice_in_dim(queries, share * picked, picked, 0).reshape(1, dest_rows, width)
    rows = lax.all_to_all(
        jnp.broadcast_to(chosen, (chips, dest_rows, width)),
        "pages", 0, 0, tiled=True, axis_index_groups=same_side,
    ).reshape(chips * dest_rows, width)

    near = pages[0]
    far = lax.ppermute(near, "tok", swap)
    near2 = lax.ppermute(near, "pages", partner)
    far2 = lax.ppermute(far, "pages", partner)
    facts = jnp.concatenate([labels[:, 0], pad_counts])
    facts2 = lax.ppermute(facts, "pages", partner)
    both = jnp.stack([facts, facts2])
    usable = page_len - both[:, -1:]
    limits = jnp.concatenate([usable - share * tokens, usable - (1 - share) * tokens], axis=1).reshape(4)
    label = both[:, :-1].reshape(2, chips, 2, shares, picked)
    label = lax.dynamic_slice(label, (0, 0, side, share, 0), (2, chips, 1, 1, picked))
    sign = jnp.repeat(2.0 * label.reshape(2, chips * picked).astype(jnp.float32) - 1.0, query_len, axis=1)

    row_count = chips * dest_rows
    block_rows = math.gcd(row_count, ROW_BLOCK)
    scratch = [] if row_count == block_rows else [pltpu.VMEM((tokens, width), jnp.float32)] * 4
    blocks, near_sum, far_sum, sent, loss = pl.pallas_call(
        functools.partial(step_body, query_len, page_len, shares),
        out_shape=(
            jax.ShapeDtypeStruct((chips, shares, dest_rows, width), jnp.bfloat16),
            jax.ShapeDtypeStruct((tokens, width), jnp.float32),
            jax.ShapeDtypeStruct((tokens, width), jnp.float32),
            jax.ShapeDtypeStruct((2 * tokens + TAIL, width), jnp.bfloat16),
            jax.ShapeDtypeStruct((8, LANES), jnp.float32),
        ),
        in_specs=[smem, vmem, vmem, vmem, vmem, vmem, vmem],
        out_specs=(vmem,) * 5,
        scratch_shapes=scratch,
        cost_estimate=pl.CostEstimate(
            flops=12 * row_count * page_len * width,
            transcendentals=2 * row_count * page_len,
            bytes_accessed=6 * row_count * width + 20 * tokens * width,
        ),
        compiler_params=params,
        name="page_step",
    )(limits, rows, near, far, near2, far2, sign)

    got = lax.ppermute(sent, "pages", partner)
    partials = lax.all_to_all(
        blocks.reshape(chips * shares, dest_rows, width),
        ("pages", "tok"), 0, 0, tiled=True, axis_index_groups=same_side_all,
    )
    merged = pl.pallas_call(
        merge_body,
        out_shape=jax.ShapeDtypeStruct((tokens + TAIL, width), jnp.bfloat16),
        in_specs=[vmem, vmem, vmem],
        out_specs=vmem,
        cost_estimate=pl.CostEstimate(flops=tokens * width, transcendentals=0, bytes_accessed=8 * tokens * width),
        compiler_params=params,
        name="merge",
    )(far_sum, loss, got)
    got2 = lax.ppermute(merged, "tok", swap)
    page_grad, page_loss = pl.pallas_call(
        last_body,
        out_shape=(
            jax.ShapeDtypeStruct((1, tokens, width), jnp.float32),
            jax.ShapeDtypeStruct((1,), jnp.float32),
        ),
        in_specs=[vmem, vmem, vmem, vmem],
        out_specs=(vmem, smem),
        cost_estimate=pl.CostEstimate(flops=2 * tokens * width, transcendentals=0, bytes_accessed=12 * tokens * width),
        compiler_params=params,
        name="page_out",
    )(near_sum, loss, got, got2)
    summed = jnp.sum(
        partials.reshape(chips, shares, dest_rows, width).astype(jnp.float32), axis=0
    ) * (width ** (-0.5))
    query_grad = summed.reshape(query_count, query_len, width)
    return query_grad, page_grad, page_loss


def solution(mesh):
    return jax.shard_map(
        device_step,
        mesh=mesh,
        in_specs=(P("pages", None, None), P("pages", "tok", None), P("pages"), P(None, "pages")),
        out_specs=(P("pages", None, None), P("pages", "tok", None), P("pages")),
        check_vma=False,
    )
```

```python
import functools
import math

import jax
import jax.numpy as jnp
from jax import lax
from jax.experimental import pallas as pl
from jax.experimental.pallas import tpu as pltpu
from jax.sharding import PartitionSpec as P


MASKED = -1.0e30
LOGIT_SPAN = 8.0
CENTRE_SHIFT = 0.5
FILL_SHARE = 0.75
LANES = 128
ROW_BLOCK = 256
TAIL = 16
VMEM_BYTES = 24 * 2**20


def over_tokens(left, right):
    return lax.dot_general(left, right, (((0,), (0,)), ((), ())), preferred_element_type=jnp.float32)


def over_features(left, right):
    return lax.dot_general(left, right, (((1,), (1,)), ((), ())), preferred_element_type=jnp.float32)


def group_sums(values, width):
    lane = lax.broadcasted_iota(jnp.int32, values.shape, 1)
    step = 1
    while step < width:
        below = pltpu.roll(values, step, 1)
        above = pltpu.roll(values, LANES - step, 1)
        values = values + jnp.where((lane & step) != 0, below, above)
        step *= 2
    return values


def loss_parts(loss):
    whole = jnp.full((TAIL, LANES), loss, jnp.float32)
    high = whole.astype(jnp.bfloat16).astype(jnp.float32)
    middle = (whole - high).astype(jnp.bfloat16).astype(jnp.float32)
    low = whole - high - middle
    lane = lax.broadcasted_iota(jnp.int32, (TAIL, LANES), 1)
    parts = jnp.where(lane == 0, high, jnp.where(lane == 1, middle, jnp.where(lane == 2, low, 0.0)))
    return parts.astype(jnp.bfloat16)


def loss_of(parts):
    return jnp.sum(parts.astype(jnp.float32)[:1])


def ask_body(queries_ref, out_ref, sems):
    copies = [
        pltpu.make_async_copy(queries_ref, out_ref.at[k], sems.at[k]) for k in range(out_ref.shape[0])
    ]
    for copy in copies:
        copy.start()
    for copy in copies:
        copy.wait()


class Page:
    def __init__(self, query_len, page_len, query_rows, near, far, limit_near, limit_far, sign):
        tokens, width = near.shape
        block_rows = query_rows.shape[0]
        pieces = block_rows // LANES
        scale = width ** (-0.5)
        rate = scale * math.log2(math.e)
        gain = LOGIT_SPAN / query_len
        centre = query_len * (CENTRE_SHIFT + math.log(FILL_SHARE * page_len))
        place = lax.broadcasted_iota(jnp.int32, (tokens, block_rows), 0)
        raw_near = jnp.where(place < limit_near, over_features(near, query_rows), MASKED)
        raw_far = jnp.where(place < limit_far, over_features(far, query_rows), MASKED)
        highest = jnp.maximum(
            jnp.max(raw_near, axis=0, keepdims=True), jnp.max(raw_far, axis=0, keepdims=True)
        )
        self.exp_near = jnp.exp2((raw_near - highest) * rate)
        self.exp_far = jnp.exp2((raw_far - highest) * rate)
        total = jnp.sum(self.exp_near, axis=0, keepdims=True) + jnp.sum(self.exp_far, axis=0, keepdims=True)

        def stacked(v):
            return jnp.concatenate([v[:, LANES * k : LANES * (k + 1)] for k in range(pieces)], axis=0)

        sums = stacked(total)
        smooth = stacked(highest) * scale + jnp.log(sums)
        similarity = group_sums(smooth, query_len)
        sign = stacked(sign)
        against = -sign * (gain * (similarity - centre))
        small = jnp.exp(-jnp.abs(against))
        losses = jnp.maximum(against, 0.0) + jnp.log1p(small)
        sigmoid = jnp.where(against >= 0.0, 1.0, small) / (1.0 + small)
        factor = (-gain * sign) * sigmoid / sums
        self.factor = jnp.concatenate([factor[k : k + 1, :] for k in range(pieces)], axis=1)
        lane = lax.broadcasted_iota(jnp.int32, losses.shape, 1)
        self.loss = jnp.sum(jnp.where(lane % query_len == 0, losses, 0.0))

    def near(self):
        return (self.exp_near * self.factor).astype(jnp.bfloat16)

    def far(self):
        return (self.exp_far * self.factor).astype(jnp.bfloat16)


def in_blocks(row_count, body):
    block_rows = math.gcd(row_count, ROW_BLOCK)
    count = row_count // block_rows
    if count == 1:
        body(0, block_rows, True)
        return

    @pl.loop(0, count)
    def _(index):
        body(index, block_rows, index == 0)


def add_to(ref, value, first):
    if first is True:
        ref[...] = value
    else:
        ref[...] = jnp.where(first, 0.0, ref[...]) + value


def step_body(
    query_len, page_len, limits_ref, rows_ref, near_ref, far_ref, near2_ref, far2_ref, sign_ref,
    blocks_ref, near_sum, near2_sum, loss_ref, held, sem,
):
    row_count, width = rows_ref.shape
    copies, dest_rows = held.shape[1:3]
    out = pltpu.make_async_copy(held, blocks_ref, sem)

    def body(index, block_rows, first):
        offset = pl.multiple_of(index * block_rows, block_rows)
        query_rows = rows_ref[pl.ds(offset, block_rows), :]
        near, far, near2, far2 = near_ref[...], far_ref[...], near2_ref[...], far2_ref[...]
        one, two = (
            Page(
                query_len, page_len, query_rows, a, b, limits_ref[2 * k], limits_ref[2 * k + 1],
                sign_ref[k : k + 1, pl.ds(offset, block_rows)],
            )
            for k, (a, b) in enumerate(((near, far), (near2, far2)))
        )
        scaled, scaled2 = one.near(), two.near()
        terms = (
            over_tokens(near, scaled) + over_tokens(far, one.far())
            + over_tokens(near2, scaled2) + over_tokens(far2, two.far())
        )
        dests = block_rows // dest_rows
        shaped = terms.T.astype(jnp.bfloat16).reshape(dests, dest_rows, width)
        for k in range(copies):
            held[pl.ds(index * dests, dests), k] = shaped
        if first is True:
            out.start()
        add_to(near_sum, jnp.dot(scaled, query_rows, preferred_element_type=jnp.float32), first)
        add_to(near2_sum, jnp.dot(scaled2, query_rows, preferred_element_type=jnp.float32), first)
        row = lax.broadcasted_iota(jnp.int32, loss_ref.shape, 0)
        add_to(loss_ref, jnp.where(row == 0, one.loss, two.loss), first)

    in_blocks(row_count, body)
    if row_count != math.gcd(row_count, ROW_BLOCK):
        out.start()
    out.wait()


def rest_body(
    query_len, page_len, limits_ref, rows_ref, near_ref, far_ref, near2_ref, far2_ref, sign_ref,
    sum_ref, sum2_ref, loss_in, near_out, sent_ref, loss_out, near_sum, near2_sum, loss_sum,
):
    row_count, width = rows_ref.shape
    tokens = near_ref.shape[0]
    scale = width ** (-0.5)

    def body(index, block_rows, first):
        offset = pl.multiple_of(index * block_rows, block_rows)
        query_rows = rows_ref[pl.ds(offset, block_rows), :]
        one, two = (
            Page(
                query_len, page_len, query_rows, a[...], b[...], limits_ref[2 * k], limits_ref[2 * k + 1],
                sign_ref[k : k + 1, pl.ds(offset, block_rows)],
            )
            for k, (a, b) in enumerate(((near_ref, far_ref), (near2_ref, far2_ref)))
        )
        add_to(near_sum, jnp.dot(one.near(), query_rows, preferred_element_type=jnp.float32), first)
        add_to(near2_sum, jnp.dot(two.near(), query_rows, preferred_element_type=jnp.float32), first)
        row = lax.broadcasted_iota(jnp.int32, loss_sum.shape, 0)
        add_to(loss_sum, jnp.where(row == 0, one.loss, two.loss), first)

    in_blocks(row_count, body)
    near_out[...] = (near_sum[...] + sum_ref[...]) * scale
    sent_ref[pl.ds(0, tokens), :] = ((near2_sum[...] + sum2_ref[...]) * scale).astype(jnp.bfloat16)
    losses = loss_in[...] + loss_sum[...]
    loss_out[...] = losses
    sent_ref[pl.ds(tokens, TAIL), :] = loss_parts(jnp.max(losses[1:2]))


def last_body(near_ref, loss_ref, got_ref, grad_ref, total_ref):
    tokens = near_ref.shape[0]
    grad_ref[0] = near_ref[...] + got_ref[pl.ds(0, tokens), :].astype(jnp.float32)
    total_ref[0] = jnp.max(loss_ref[0:1, :]) + loss_of(got_ref[pl.ds(tokens, TAIL), :])


def device_step(queries, pages, pad_counts, labels):
    query_count, query_len, width = queries.shape
    _, tokens, _ = pages.shape
    owners = lax.axis_size("pages")
    shares = lax.axis_size("tok")
    if shares != 2 or query_count % shares or owners % 2:
        raise ValueError("unsupported split")
    share = lax.axis_index("tok")
    side = lax.axis_index("pages") % 2
    page_len = tokens * shares
    picked = query_count // shares
    dest_rows = picked * query_len
    chips = owners // 2
    swap = [(0, 1), (1, 0)]
    partner = [(i, i ^ 1) for i in range(owners)]
    turn = chips // 2
    order = [(j + turn) % chips for j in range(chips)]
    same_side = [[2 * j + c for j in order] for c in range(2)]
    same_side_all = [
        [(2 * j + c) * shares + k for j in order for k in range(shares)] for c in range(2)
    ]
    vmem = pl.BlockSpec(memory_space=pltpu.VMEM)
    smem = pl.BlockSpec(memory_space=pltpu.SMEM)
    anywhere = pl.BlockSpec(memory_space=pl.ANY)
    params = pltpu.CompilerParams(vmem_limit_bytes=VMEM_BYTES)

    asked = pl.pallas_call(
        ask_body,
        out_shape=jax.ShapeDtypeStruct((chips, query_count, query_len, width), queries.dtype),
        in_specs=[anywhere],
        out_specs=anywhere,
        scratch_shapes=[pltpu.SemaphoreType.DMA((chips,))],
        compiler_params=params,
        name="ask_copies",
    )(queries)
    gathered = lax.all_to_all(
        asked.reshape(chips, query_count * query_len, width),
        "pages", 0, 0, tiled=True, axis_index_groups=same_side,
    ).reshape(chips, shares, dest_rows, width)

    near = pages[0]
    far = lax.ppermute(near, "tok", swap)
    near2 = lax.ppermute(near, "pages", partner)
    far2 = lax.ppermute(far, "pages", partner)
    facts = jnp.concatenate([labels[:, 0], pad_counts])
    facts2 = lax.ppermute(facts, "pages", partner)
    both = jnp.stack([facts, facts2])
    usable = page_len - both[:, -1:]
    limits = jnp.concatenate([usable - share * tokens, usable - (1 - share) * tokens], axis=1).reshape(4)
    label = jnp.roll(both[:, :-1].reshape(2, chips, 2, shares, picked), -turn, axis=1)
    label = 2.0 * lax.dynamic_index_in_dim(label, side, 2, False).astype(jnp.float32) - 1.0

    def of_share(index):
        rows = lax.dynamic_index_in_dim(gathered, index, 1, False).reshape(row_count, width)
        sign = lax.dynamic_index_in_dim(label, index, 2, False).reshape(2, chips * picked)
        return rows, jnp.repeat(sign, query_len, axis=1)

    row_count = chips * dest_rows
    rows, sign = of_share(share)
    rows_b, sign_b = of_share(1 - share)
    half = jax.ShapeDtypeStruct((tokens, width), jnp.float32)
    lane_row = jax.ShapeDtypeStruct((8, LANES), jnp.float32)
    blocks, near_sum, near2_sum, loss = pl.pallas_call(
        functools.partial(step_body, query_len, page_len),
        out_shape=(
            jax.ShapeDtypeStruct((chips, shares, dest_rows, width), jnp.bfloat16), half, half, lane_row,
        ),
        in_specs=[smem, vmem, vmem, vmem, vmem, vmem, vmem],
        out_specs=(anywhere, vmem, vmem, vmem),
        scratch_shapes=[
            pltpu.VMEM((chips, shares, dest_rows, width), jnp.bfloat16),
            pltpu.SemaphoreType.DMA,
        ],
        cost_estimate=pl.CostEstimate(
            flops=10 * row_count * page_len * width,
            transcendentals=2 * row_count * page_len,
            bytes_accessed=6 * row_count * width + 20 * tokens * width,
        ),
        compiler_params=params,
        name="page_step",
    )(limits, rows, near, far, near2, far2, sign)

    partials = lax.all_to_all(
        blocks.reshape(chips * shares, dest_rows, width),
        ("pages", "tok"), 0, 0, tiled=True, axis_index_groups=same_side_all,
    )
    near_sum, sent, loss = pl.pallas_call(
        functools.partial(rest_body, query_len, page_len),
        out_shape=(half, jax.ShapeDtypeStruct((tokens + TAIL, width), jnp.bfloat16), lane_row),
        in_specs=[smem] + [vmem] * 9,
        out_specs=(vmem,) * 3,
        scratch_shapes=[pltpu.VMEM((tokens, width), jnp.float32)] * 2 + [pltpu.VMEM((8, LANES), jnp.float32)],
        cost_estimate=pl.CostEstimate(
            flops=6 * row_count * page_len * width,
            transcendentals=2 * row_count * page_len,
            bytes_accessed=2 * row_count * width + 20 * tokens * width,
        ),
        compiler_params=params,
        name="page_rest",
    )(limits, rows_b, near, far, near2, far2, sign_b, near_sum, near2_sum, loss)
    got = lax.ppermute(sent, "pages", partner)
    page_grad, page_loss = pl.pallas_call(
        last_body,
        out_shape=(
            jax.ShapeDtypeStruct((1, tokens, width), jnp.float32),
            jax.ShapeDtypeStruct((1,), jnp.float32),
        ),
        in_specs=[vmem, vmem, vmem],
        out_specs=(vmem, smem),
        cost_estimate=pl.CostEstimate(flops=2 * tokens * width, transcendentals=0, bytes_accessed=12 * tokens * width),
        compiler_params=params,
        name="page_out",
    )(near_sum, loss, got)
    summed = jnp.sum(
        partials.reshape(chips, shares, dest_rows, width).astype(jnp.float32), axis=0
    ) * (width ** (-0.5))
    query_grad = summed.reshape(query_count, query_len, width)
    return query_grad, page_grad, page_loss


def solution(mesh):
    return jax.shard_map(
        device_step,
        mesh=mesh,
        in_specs=(P("pages", None, None), P("pages", "tok", None), P("pages"), P(None, "pages")),
        out_specs=(P("pages", None, None), P("pages", "tok", None), P("pages")),
        check_vma=False,
    )
```

```python
import functools
import math

import jax
import jax.numpy as jnp
from jax import lax
from jax.experimental import pallas as pl
from jax.experimental.pallas import tpu as pltpu
from jax.sharding import PartitionSpec as P


MASKED = -1.0e30
LOGIT_SPAN = 8.0
CENTRE_SHIFT = 0.5
FILL_SHARE = 0.75
LANES = 128
ROW_BLOCK = 256
TAIL = 16
SHIFT = 1
VMEM_BYTES = 24 * 2**20


def over_tokens(left, right):
    return lax.dot_general(left, right, (((0,), (0,)), ((), ())), preferred_element_type=jnp.float32)


def over_features(left, right):
    return lax.dot_general(left, right, (((1,), (1,)), ((), ())), preferred_element_type=jnp.float32)


def group_sums(values, width):
    lane = lax.broadcasted_iota(jnp.int32, values.shape, 1)
    step = 1
    while step < width:
        below = pltpu.roll(values, step, 1)
        above = pltpu.roll(values, LANES - step, 1)
        values = values + jnp.where((lane & step) != 0, below, above)
        step *= 2
    return values


def loss_parts(loss):
    whole = jnp.full((TAIL, LANES), loss, jnp.float32)
    high = whole.astype(jnp.bfloat16).astype(jnp.float32)
    middle = (whole - high).astype(jnp.bfloat16).astype(jnp.float32)
    low = whole - high - middle
    lane = lax.broadcasted_iota(jnp.int32, (TAIL, LANES), 1)
    parts = jnp.where(lane == 0, high, jnp.where(lane == 1, middle, jnp.where(lane == 2, low, 0.0)))
    return parts.astype(jnp.bfloat16)


def loss_of(parts):
    return jnp.sum(parts.astype(jnp.float32)[:1])


def ask_body(queries_ref, out_ref, sems):
    copies = [
        pltpu.make_async_copy(queries_ref, out_ref.at[k], sems.at[k]) for k in range(out_ref.shape[0])
    ]
    for copy in copies:
        copy.start()
    for copy in copies:
        copy.wait()


class Page:
    def __init__(self, query_len, page_len, query_rows, near, far, limit_near, limit_far, sign):
        tokens, width = near.shape
        block_rows = query_rows.shape[0]
        pieces = block_rows // LANES
        scale = width ** (-0.5)
        rate = scale * math.log2(math.e)
        gain = LOGIT_SPAN / query_len
        centre = query_len * (CENTRE_SHIFT + math.log(FILL_SHARE * page_len))
        place = lax.broadcasted_iota(jnp.int32, (tokens, block_rows), 0)
        raw_near = jnp.where(place < limit_near, over_features(near, query_rows), MASKED)
        raw_far = jnp.where(place < limit_far, over_features(far, query_rows), MASKED)
        highest = jnp.maximum(
            jnp.max(raw_near, axis=0, keepdims=True), jnp.max(raw_far, axis=0, keepdims=True)
        )
        self.exp_near = jnp.exp2((raw_near - highest) * rate)
        self.exp_far = jnp.exp2((raw_far - highest) * rate)
        total = jnp.sum(self.exp_near, axis=0, keepdims=True) + jnp.sum(self.exp_far, axis=0, keepdims=True)

        def stacked(v):
            return jnp.concatenate([v[:, LANES * k : LANES * (k + 1)] for k in range(pieces)], axis=0)

        sums = stacked(total)
        smooth = stacked(highest) * scale + jnp.log(sums)
        similarity = group_sums(smooth, query_len)
        sign = stacked(sign)
        against = -sign * (gain * (similarity - centre))
        small = jnp.exp(-jnp.abs(against))
        losses = jnp.maximum(against, 0.0) + jnp.log1p(small)
        sigmoid = jnp.where(against >= 0.0, 1.0, small) / (1.0 + small)
        factor = (-gain * sign) * sigmoid / sums
        self.factor = jnp.concatenate([factor[k : k + 1, :] for k in range(pieces)], axis=1)
        lane = lax.broadcasted_iota(jnp.int32, losses.shape, 1)
        self.loss = jnp.sum(jnp.where(lane % query_len == 0, losses, 0.0))

    def near(self):
        return (self.exp_near * self.factor).astype(jnp.bfloat16)

    def far(self):
        return (self.exp_far * self.factor).astype(jnp.bfloat16)


def in_blocks(row_count, body):
    block_rows = math.gcd(row_count, ROW_BLOCK)
    count = row_count // block_rows
    if count == 1:
        body(0, block_rows, True)
        return

    @pl.loop(0, count)
    def _(index):
        body(index, block_rows, index == 0)


def add_to(ref, value, first):
    if first is True:
        ref[...] = value
    else:
        ref[...] = jnp.where(first, 0.0, ref[...]) + value


def step_body(
    query_len, page_len, limits_ref, rows_ref, near_ref, far_ref, near2_ref, far2_ref, sign_ref,
    blocks_ref, near_sum, near2_sum, loss_ref, held, sem,
):
    row_count, width = rows_ref.shape
    copies, dest_rows = held.shape[1:3]
    out = pltpu.make_async_copy(held, blocks_ref, sem)

    def body(index, block_rows, first):
        offset = pl.multiple_of(index * block_rows, block_rows)
        query_rows = rows_ref[pl.ds(offset, block_rows), :]
        near, far, near2, far2 = near_ref[...], far_ref[...], near2_ref[...], far2_ref[...]
        one, two = (
            Page(
                query_len, page_len, query_rows, a, b, limits_ref[2 * k], limits_ref[2 * k + 1],
                sign_ref[k : k + 1, pl.ds(offset, block_rows)],
            )
            for k, (a, b) in enumerate(((near, far), (near2, far2)))
        )
        scaled, scaled2 = one.near(), two.near()
        terms = (
            over_tokens(near, scaled) + over_tokens(far, one.far())
            + over_tokens(near2, scaled2) + over_tokens(far2, two.far())
        )
        dests = block_rows // dest_rows
        shaped = terms.T.astype(jnp.bfloat16).reshape(dests, dest_rows, width)
        for d in range(dests):
            place = lax.rem(index * dests + d + held.shape[0] - SHIFT, held.shape[0])
            for k in range(copies):
                held[place, k] = shaped[d]
        if first is True:
            out.start()
        add_to(near_sum, jnp.dot(scaled, query_rows, preferred_element_type=jnp.float32), first)
        add_to(near2_sum, jnp.dot(scaled2, query_rows, preferred_element_type=jnp.float32), first)
        row = lax.broadcasted_iota(jnp.int32, loss_ref.shape, 0)
        add_to(loss_ref, jnp.where(row == 0, one.loss, two.loss), first)

    in_blocks(row_count, body)
    if row_count != math.gcd(row_count, ROW_BLOCK):
        out.start()
    out.wait()


def rest_body(
    query_len, page_len, limits_ref, rows_ref, near_ref, far_ref, near2_ref, far2_ref, sign_ref,
    sum_ref, sum2_ref, loss_in, near_out, sent_ref, loss_out, near_sum, near2_sum, loss_sum,
):
    row_count, width = rows_ref.shape
    tokens = near_ref.shape[0]
    scale = width ** (-0.5)

    def body(index, block_rows, first):
        offset = pl.multiple_of(index * block_rows, block_rows)
        query_rows = rows_ref[pl.ds(offset, block_rows), :]
        one, two = (
            Page(
                query_len, page_len, query_rows, a[...], b[...], limits_ref[2 * k], limits_ref[2 * k + 1],
                sign_ref[k : k + 1, pl.ds(offset, block_rows)],
            )
            for k, (a, b) in enumerate(((near_ref, far_ref), (near2_ref, far2_ref)))
        )
        add_to(near_sum, jnp.dot(one.near(), query_rows, preferred_element_type=jnp.float32), first)
        add_to(near2_sum, jnp.dot(two.near(), query_rows, preferred_element_type=jnp.float32), first)
        row = lax.broadcasted_iota(jnp.int32, loss_sum.shape, 0)
        add_to(loss_sum, jnp.where(row == 0, one.loss, two.loss), first)

    in_blocks(row_count, body)
    near_out[...] = (near_sum[...] + sum_ref[...]) * scale
    sent_ref[pl.ds(0, tokens), :] = ((near2_sum[...] + sum2_ref[...]) * scale).astype(jnp.bfloat16)
    losses = loss_in[...] + loss_sum[...]
    loss_out[...] = losses
    sent_ref[pl.ds(tokens, TAIL), :] = loss_parts(jnp.max(losses[1:2]))


def last_body(near_ref, loss_ref, got_ref, grad_ref, total_ref):
    tokens = near_ref.shape[0]
    grad_ref[0] = near_ref[...] + got_ref[pl.ds(0, tokens), :].astype(jnp.float32)
    total_ref[0] = jnp.max(loss_ref[0:1, :]) + loss_of(got_ref[pl.ds(tokens, TAIL), :])


def device_step(queries, pages, pad_counts, labels):
    query_count, query_len, width = queries.shape
    _, tokens, _ = pages.shape
    owners = lax.axis_size("pages")
    shares = lax.axis_size("tok")
    if shares != 2 or query_count % shares or owners % 2:
        raise ValueError("unsupported split")
    share = lax.axis_index("tok")
    side = lax.axis_index("pages") % 2
    page_len = tokens * shares
    picked = query_count // shares
    dest_rows = picked * query_len
    chips = owners // 2
    swap = [(0, 1), (1, 0)]
    partner = [(i, i ^ 1) for i in range(owners)]
    turn = chips // 2
    order = [(j + turn) % chips for j in range(chips)]
    same_side = [[2 * j + c for j in order] for c in range(2)]
    later = order[SHIFT:] + order[:SHIFT]
    same_side_all = [
        [(2 * j + c) * shares + k for j in later for k in range(shares)] for c in range(2)
    ]
    vmem = pl.BlockSpec(memory_space=pltpu.VMEM)
    smem = pl.BlockSpec(memory_space=pltpu.SMEM)
    anywhere = pl.BlockSpec(memory_space=pl.ANY)
    params = pltpu.CompilerParams(vmem_limit_bytes=VMEM_BYTES)

    asked = pl.pallas_call(
        ask_body,
        out_shape=jax.ShapeDtypeStruct((chips, query_count, query_len, width), queries.dtype),
        in_specs=[anywhere],
        out_specs=anywhere,
        scratch_shapes=[pltpu.SemaphoreType.DMA((chips,))],
        compiler_params=params,
        name="ask_copies",
    )(queries)
    gathered = lax.all_to_all(
        asked.reshape(chips, query_count * query_len, width),
        "pages", 0, 0, tiled=True, axis_index_groups=same_side,
    ).reshape(chips, shares, dest_rows, width)

    near = pages[0]
    far = lax.ppermute(near, "tok", swap)
    near2 = lax.ppermute(near, "pages", partner)
    far2 = lax.ppermute(far, "pages", partner)
    facts = jnp.concatenate([labels[:, 0], pad_counts])
    facts2 = lax.ppermute(facts, "pages", partner)
    both = jnp.stack([facts, facts2])
    usable = page_len - both[:, -1:]
    limits = jnp.concatenate([usable - share * tokens, usable - (1 - share) * tokens], axis=1).reshape(4)
    label = jnp.roll(both[:, :-1].reshape(2, chips, 2, shares, picked), -turn, axis=1)
    label = 2.0 * lax.dynamic_index_in_dim(label, side, 2, False).astype(jnp.float32) - 1.0

    def of_share(index):
        rows = lax.dynamic_index_in_dim(gathered, index, 1, False).reshape(row_count, width)
        sign = lax.dynamic_index_in_dim(label, index, 2, False).reshape(2, chips * picked)
        return rows, jnp.repeat(sign, query_len, axis=1)

    row_count = chips * dest_rows
    rows, sign = of_share(share)
    rows_b, sign_b = of_share(1 - share)
    half = jax.ShapeDtypeStruct((tokens, width), jnp.float32)
    lane_row = jax.ShapeDtypeStruct((8, LANES), jnp.float32)
    blocks, near_sum, near2_sum, loss = pl.pallas_call(
        functools.partial(step_body, query_len, page_len),
        out_shape=(
            jax.ShapeDtypeStruct((chips, shares, dest_rows, width), jnp.bfloat16), half, half, lane_row,
        ),
        in_specs=[smem, vmem, vmem, vmem, vmem, vmem, vmem],
        out_specs=(anywhere, vmem, vmem, vmem),
        scratch_shapes=[
            pltpu.VMEM((chips, shares, dest_rows, width), jnp.bfloat16),
            pltpu.SemaphoreType.DMA,
        ],
        cost_estimate=pl.CostEstimate(
            flops=10 * row_count * page_len * width,
            transcendentals=2 * row_count * page_len,
            bytes_accessed=6 * row_count * width + 20 * tokens * width,
        ),
        compiler_params=params,
        name="page_step",
    )(limits, rows, near, far, near2, far2, sign)

    partials = lax.all_to_all(
        blocks.reshape(chips * shares, dest_rows, width),
        ("pages", "tok"), 0, 0, tiled=True, axis_index_groups=same_side_all,
    )
    near_sum, sent, loss = pl.pallas_call(
        functools.partial(rest_body, query_len, page_len),
        out_shape=(half, jax.ShapeDtypeStruct((tokens + TAIL, width), jnp.bfloat16), lane_row),
        in_specs=[smem] + [vmem] * 9,
        out_specs=(vmem,) * 3,
        scratch_shapes=[pltpu.VMEM((tokens, width), jnp.float32)] * 2 + [pltpu.VMEM((8, LANES), jnp.float32)],
        cost_estimate=pl.CostEstimate(
            flops=6 * row_count * page_len * width,
            transcendentals=2 * row_count * page_len,
            bytes_accessed=2 * row_count * width + 20 * tokens * width,
        ),
        compiler_params=params,
        name="page_rest",
    )(limits, rows_b, near, far, near2, far2, sign_b, near_sum, near2_sum, loss)
    got = lax.ppermute(sent, "pages", partner)
    page_grad, page_loss = pl.pallas_call(
        last_body,
        out_shape=(
            jax.ShapeDtypeStruct((1, tokens, width), jnp.float32),
            jax.ShapeDtypeStruct((1,), jnp.float32),
        ),
        in_specs=[vmem, vmem, vmem],
        out_specs=(vmem, smem),
        cost_estimate=pl.CostEstimate(flops=2 * tokens * width, transcendentals=0, bytes_accessed=12 * tokens * width),
        compiler_params=params,
        name="page_out",
    )(near_sum, loss, got)
    summed = jnp.sum(
        partials.reshape(chips, shares, dest_rows, width).astype(jnp.float32), axis=0
    ) * (width ** (-0.5))
    query_grad = summed.reshape(query_count, query_len, width)
    return query_grad, page_grad, page_loss


def solution(mesh):
    return jax.shard_map(
        device_step,
        mesh=mesh,
        in_specs=(P("pages", None, None), P("pages", "tok", None), P("pages"), P(None, "pages")),
        out_specs=(P("pages", None, None), P("pages", "tok", None), P("pages")),
        check_vma=False,
    )
```

```python
import functools
import math

import jax
import jax.numpy as jnp
from jax import lax
from jax.experimental import pallas as pl
from jax.experimental.pallas import tpu as pltpu
from jax.sharding import PartitionSpec as P


MASKED = -1.0e30
LOGIT_SPAN = 8.0
CENTRE_SHIFT = 0.5
FILL_SHARE = 0.75
LANES = 128
ROW_BLOCK = 256
TAIL = 16
SHIFT = 1
VMEM_BYTES = 24 * 2**20


def over_tokens(left, right):
    return lax.dot_general(left, right, (((0,), (0,)), ((), ())), preferred_element_type=jnp.float32)


def over_features(left, right):
    return lax.dot_general(left, right, (((1,), (1,)), ((), ())), preferred_element_type=jnp.float32)


def group_sums(values, width):
    lane = lax.broadcasted_iota(jnp.int32, values.shape, 1)
    step = 1
    while step < width:
        below = pltpu.roll(values, step, 1)
        above = pltpu.roll(values, LANES - step, 1)
        values = values + jnp.where((lane & step) != 0, below, above)
        step *= 2
    return values


def loss_parts(loss):
    whole = jnp.full((TAIL, LANES), loss, jnp.float32)
    high = whole.astype(jnp.bfloat16).astype(jnp.float32)
    middle = (whole - high).astype(jnp.bfloat16).astype(jnp.float32)
    low = whole - high - middle
    lane = lax.broadcasted_iota(jnp.int32, (TAIL, LANES), 1)
    parts = jnp.where(lane == 0, high, jnp.where(lane == 1, middle, jnp.where(lane == 2, low, 0.0)))
    return parts.astype(jnp.bfloat16)


def loss_of(parts):
    return jnp.sum(parts.astype(jnp.float32)[:1])


def ask_body(queries_ref, out_ref, sems):
    copies = [
        pltpu.make_async_copy(queries_ref, out_ref.at[k], sems.at[k]) for k in range(out_ref.shape[0])
    ]
    for copy in copies:
        copy.start()
    for copy in copies:
        copy.wait()


class Page:
    def __init__(self, query_len, page_len, query_rows, near, far, bias_near, bias_far, sign):
        _, width = near.shape
        block_rows = query_rows.shape[0]
        pieces = block_rows // LANES
        scale = width ** (-0.5)
        rate = scale * math.log2(math.e)
        gain = LOGIT_SPAN / query_len
        centre = query_len * (CENTRE_SHIFT + math.log(FILL_SHARE * page_len))
        lane = lax.broadcasted_iota(jnp.int32, (block_rows, LANES), 1)
        one = jnp.where(lane == 0, 1.0, 0.0).astype(jnp.bfloat16)
        wide_rows = jnp.concatenate([query_rows, one], axis=1)
        raw_near = over_features(jnp.concatenate([near, bias_near], axis=1), wide_rows)
        raw_far = over_features(jnp.concatenate([far, bias_far], axis=1), wide_rows)
        highest = jnp.maximum(
            jnp.max(raw_near, axis=0, keepdims=True), jnp.max(raw_far, axis=0, keepdims=True)
        )
        self.exp_near = jnp.exp2((raw_near - highest) * rate)
        self.exp_far = jnp.exp2((raw_far - highest) * rate)
        total = jnp.sum(self.exp_near, axis=0, keepdims=True) + jnp.sum(self.exp_far, axis=0, keepdims=True)

        def stacked(v):
            return jnp.concatenate([v[:, LANES * k : LANES * (k + 1)] for k in range(pieces)], axis=0)

        sums = stacked(total)
        smooth = stacked(highest) * scale + jnp.log(sums)
        similarity = group_sums(smooth, query_len)
        sign = stacked(sign)
        against = -sign * (gain * (similarity - centre))
        small = jnp.exp(-jnp.abs(against))
        losses = jnp.maximum(against, 0.0) + jnp.log1p(small)
        sigmoid = jnp.where(against >= 0.0, 1.0, small) / (1.0 + small)
        factor = (-gain * sign) * sigmoid / sums
        self.factor = jnp.concatenate([factor[k : k + 1, :] for k in range(pieces)], axis=1)
        lane = lax.broadcasted_iota(jnp.int32, losses.shape, 1)
        self.loss = jnp.sum(jnp.where(lane % query_len == 0, losses, 0.0))

    def near(self):
        return (self.exp_near * self.factor).astype(jnp.bfloat16)

    def query_terms(self, near, far):
        terms = over_tokens(near, self.exp_near.astype(jnp.bfloat16))
        return (terms + over_tokens(far, self.exp_far.astype(jnp.bfloat16))) * self.factor


def in_blocks(row_count, body):
    block_rows = math.gcd(row_count, ROW_BLOCK)
    count = row_count // block_rows
    if count == 1:
        body(0, block_rows, True)
        return

    @pl.loop(0, count)
    def _(index):
        body(index, block_rows, index == 0)


def add_to(ref, value, first):
    if first is True:
        ref[...] = value
    else:
        ref[...] = jnp.where(first, 0.0, ref[...]) + value


def step_body(
    query_len, page_len, bias_ref, rows_ref, near_ref, far_ref, near2_ref, far2_ref, sign_ref,
    blocks_ref, sums_ref, loss_ref, held, kept, factors, sem,
):
    row_count, width = rows_ref.shape
    copies, dest_rows = held.shape[1:3]
    out = pltpu.make_async_copy(held, blocks_ref, sem)

    def body(index, block_rows, first):
        offset = pl.multiple_of(index * block_rows, block_rows)
        query_rows = rows_ref[pl.ds(offset, block_rows), :]
        near, far, near2, far2 = near_ref[...], far_ref[...], near2_ref[...], far2_ref[...]
        one, two = (
            Page(
                query_len, page_len, query_rows, a, b, bias_ref[2 * k], bias_ref[2 * k + 1],
                sign_ref[k : k + 1, pl.ds(offset, block_rows)],
            )
            for k, (a, b) in enumerate(((near, far), (near2, far2)))
        )
        terms = one.query_terms(near, far) + two.query_terms(near2, far2)
        dests = block_rows // dest_rows
        shaped = terms.T.astype(jnp.bfloat16).reshape(dests, dest_rows, width)
        for d in range(dests):
            place = lax.rem(index * dests + d + held.shape[0] - SHIFT, held.shape[0])
            for k in range(copies):
                held[place, k] = shaped[d]
        for k, page in enumerate((one, two)):
            kept[k] = page.exp_near
            factors[k] = page.factor
        if first is True:
            out.start()
        row = lax.broadcasted_iota(jnp.int32, loss_ref.shape, 0)
        add_to(loss_ref, jnp.where(row == 0, one.loss, two.loss), first)

        @pl.loop(0, 2)
        def _(page):
            scaled = (kept[page] * factors[page]).astype(jnp.bfloat16)
            add_to(
                sums_ref.at[page],
                jnp.dot(scaled, rows_ref[pl.ds(offset, block_rows), :], preferred_element_type=jnp.float32),
                first,
            )

    in_blocks(row_count, body)
    if row_count != math.gcd(row_count, ROW_BLOCK):
        out.start()
    out.wait()


def rest_body(
    query_len, page_len, bias_ref, rows_ref, near_ref, far_ref, near2_ref, far2_ref, sign_ref,
    sums_ref, loss_in, near_out, sent_ref, loss_out, near_sum, near2_sum, loss_sum,
):
    row_count, width = rows_ref.shape
    tokens = near_ref.shape[0]
    scale = width ** (-0.5)

    def body(index, block_rows, first):
        offset = pl.multiple_of(index * block_rows, block_rows)
        query_rows = rows_ref[pl.ds(offset, block_rows), :]
        one, two = (
            Page(
                query_len, page_len, query_rows, a[...], b[...], bias_ref[2 * k], bias_ref[2 * k + 1],
                sign_ref[k : k + 1, pl.ds(offset, block_rows)],
            )
            for k, (a, b) in enumerate(((near_ref, far_ref), (near2_ref, far2_ref)))
        )
        add_to(near_sum, jnp.dot(one.near(), query_rows, preferred_element_type=jnp.float32), first)
        add_to(near2_sum, jnp.dot(two.near(), query_rows, preferred_element_type=jnp.float32), first)
        row = lax.broadcasted_iota(jnp.int32, loss_sum.shape, 0)
        add_to(loss_sum, jnp.where(row == 0, one.loss, two.loss), first)

    in_blocks(row_count, body)
    near_out[...] = (near_sum[...] + sums_ref[0]) * scale
    sent_ref[pl.ds(0, tokens), :] = ((near2_sum[...] + sums_ref[1]) * scale).astype(jnp.bfloat16)
    losses = loss_in[...] + loss_sum[...]
    loss_out[...] = losses
    sent_ref[pl.ds(tokens, TAIL), :] = loss_parts(jnp.max(losses[1:2]))


def bias_body(limits_ref, bias_ref):
    shape = bias_ref.shape[1:]
    row = lax.broadcasted_iota(jnp.int32, shape, 0)
    lane = lax.broadcasted_iota(jnp.int32, shape, 1)
    for k in range(bias_ref.shape[0]):
        padding = (row >= limits_ref[k]) & (lane == 0)
        bias_ref[k] = jnp.where(padding, MASKED, 0.0).astype(jnp.bfloat16)


def last_body(near_ref, loss_ref, got_ref, grad_ref, total_ref):
    tokens = near_ref.shape[0]
    grad_ref[0] = near_ref[...] + got_ref[pl.ds(0, tokens), :].astype(jnp.float32)
    total_ref[0] = jnp.max(loss_ref[0:1, :]) + loss_of(got_ref[pl.ds(tokens, TAIL), :])


def device_step(queries, pages, pad_counts, labels):
    query_count, query_len, width = queries.shape
    _, tokens, _ = pages.shape
    owners = lax.axis_size("pages")
    shares = lax.axis_size("tok")
    if shares != 2 or query_count % shares or owners % 2:
        raise ValueError("unsupported split")
    share = lax.axis_index("tok")
    side = lax.axis_index("pages") % 2
    page_len = tokens * shares
    picked = query_count // shares
    dest_rows = picked * query_len
    chips = owners // 2
    swap = [(0, 1), (1, 0)]
    partner = [(i, i ^ 1) for i in range(owners)]
    turn = chips // 2
    order = [(j + turn) % chips for j in range(chips)]
    same_side = [[2 * j + c for j in order] for c in range(2)]
    later = order[SHIFT:] + order[:SHIFT]
    same_side_all = [
        [(2 * j + c) * shares + k for j in later for k in range(shares)] for c in range(2)
    ]
    vmem = pl.BlockSpec(memory_space=pltpu.VMEM)
    smem = pl.BlockSpec(memory_space=pltpu.SMEM)
    anywhere = pl.BlockSpec(memory_space=pl.ANY)
    params = pltpu.CompilerParams(vmem_limit_bytes=VMEM_BYTES)

    asked = pl.pallas_call(
        ask_body,
        out_shape=jax.ShapeDtypeStruct((chips, query_count, query_len, width), queries.dtype),
        in_specs=[anywhere],
        out_specs=anywhere,
        scratch_shapes=[pltpu.SemaphoreType.DMA((chips,))],
        compiler_params=params,
        name="ask_copies",
    )(queries)
    gathered = lax.all_to_all(
        asked.reshape(chips, query_count * query_len, width),
        "pages", 0, 0, tiled=True, axis_index_groups=same_side,
    ).reshape(chips, shares, dest_rows, width)

    near = pages[0]
    far = lax.ppermute(near, "tok", swap)
    near2 = lax.ppermute(near, "pages", partner)
    far2 = lax.ppermute(far, "pages", partner)
    facts = jnp.concatenate([labels[:, 0], pad_counts])
    facts2 = lax.ppermute(facts, "pages", partner)
    both = jnp.stack([facts, facts2])
    usable = page_len - both[:, -1:]
    limits = jnp.concatenate([usable - share * tokens, usable - (1 - share) * tokens], axis=1).reshape(4)
    label = jnp.roll(both[:, :-1].reshape(2, chips, 2, shares, picked), -turn, axis=1)
    label = 2.0 * lax.dynamic_index_in_dim(label, side, 2, False).astype(jnp.float32) - 1.0

    def of_share(index):
        rows = lax.dynamic_index_in_dim(gathered, index, 1, False).reshape(row_count, width)
        sign = lax.dynamic_index_in_dim(label, index, 2, False).reshape(2, chips * picked)
        return rows, jnp.repeat(sign, query_len, axis=1)

    row_count = chips * dest_rows
    rows, sign = of_share(share)
    rows_b, sign_b = of_share(1 - share)
    half = jax.ShapeDtypeStruct((tokens, width), jnp.float32)
    lane_row = jax.ShapeDtypeStruct((8, LANES), jnp.float32)
    bias = pl.pallas_call(
        bias_body,
        out_shape=jax.ShapeDtypeStruct((4, tokens, LANES), jnp.bfloat16),
        in_specs=[smem],
        out_specs=vmem,
        cost_estimate=pl.CostEstimate(flops=0, transcendentals=0, bytes_accessed=8 * tokens * width),
        compiler_params=params,
        name="page_bias",
    )(limits)
    block_rows = math.gcd(row_count, ROW_BLOCK)
    blocks, sums, loss = pl.pallas_call(
        functools.partial(step_body, query_len, page_len),
        out_shape=(
            jax.ShapeDtypeStruct((chips, shares, dest_rows, width), jnp.bfloat16),
            jax.ShapeDtypeStruct((2, tokens, width), jnp.float32),
            lane_row,
        ),
        in_specs=[vmem] * 7,
        out_specs=(anywhere, vmem, vmem),
        scratch_shapes=[
            pltpu.VMEM((chips, shares, dest_rows, width), jnp.bfloat16),
            pltpu.VMEM((2, tokens, block_rows), jnp.float32),
            pltpu.VMEM((2, 1, block_rows), jnp.float32),
            pltpu.SemaphoreType.DMA,
        ],
        cost_estimate=pl.CostEstimate(
            flops=10 * row_count * page_len * width,
            transcendentals=2 * row_count * page_len,
            bytes_accessed=6 * row_count * width + 20 * tokens * width,
        ),
        compiler_params=params,
        name="page_step",
    )(bias, rows, near, far, near2, far2, sign)

    partials = lax.all_to_all(
        blocks.reshape(chips * shares, dest_rows, width),
        ("pages", "tok"), 0, 0, tiled=True, axis_index_groups=same_side_all,
    )
    near_sum, sent, loss = pl.pallas_call(
        functools.partial(rest_body, query_len, page_len),
        out_shape=(half, jax.ShapeDtypeStruct((tokens + TAIL, width), jnp.bfloat16), lane_row),
        in_specs=[vmem] * 9,
        out_specs=(vmem,) * 3,
        scratch_shapes=[pltpu.VMEM((tokens, width), jnp.float32)] * 2 + [pltpu.VMEM((8, LANES), jnp.float32)],
        cost_estimate=pl.CostEstimate(
            flops=6 * row_count * page_len * width,
            transcendentals=2 * row_count * page_len,
            bytes_accessed=2 * row_count * width + 20 * tokens * width,
        ),
        compiler_params=params,
        name="page_rest",
    )(bias, rows_b, near, far, near2, far2, sign_b, sums, loss)
    got = lax.ppermute(sent, "pages", partner)
    page_grad, page_loss = pl.pallas_call(
        last_body,
        out_shape=(
            jax.ShapeDtypeStruct((1, tokens, width), jnp.float32),
            jax.ShapeDtypeStruct((1,), jnp.float32),
        ),
        in_specs=[vmem, vmem, vmem],
        out_specs=(vmem, smem),
        cost_estimate=pl.CostEstimate(flops=2 * tokens * width, transcendentals=0, bytes_accessed=12 * tokens * width),
        compiler_params=params,
        name="page_out",
    )(near_sum, loss, got)
    summed = jnp.sum(
        partials.reshape(chips, shares, dest_rows, width).astype(jnp.float32), axis=0
    ) * (width ** (-0.5))
    query_grad = summed.reshape(query_count, query_len, width)
    return query_grad, page_grad, page_loss


def solution(mesh):
    return jax.shard_map(
        device_step,
        mesh=mesh,
        in_specs=(P("pages", None, None), P("pages", "tok", None), P("pages"), P(None, "pages")),
        out_specs=(P("pages", None, None), P("pages", "tok", None), P("pages")),
        check_vma=False,
    )
```

```python
import functools
import math

import jax
import jax.numpy as jnp
from jax import lax
from jax.experimental import pallas as pl
from jax.experimental.pallas import tpu as pltpu
from jax.sharding import PartitionSpec as P


MASKED = -1.0e30
LOGIT_SPAN = 8.0
CENTRE_SHIFT = 0.5
FILL_SHARE = 0.75
LANES = 128
ROW_BLOCK = 256
TAIL = 16
SHIFT = 1
VMEM_BYTES = 24 * 2**20


def chip_at(place, chips):
    half = chips // 2
    step = 1 if half % 2 else 2
    down = place - half
    if isinstance(place, int):
        return place + half if down < 0 else step * (half // step - 1 - down // step) + down % step
    down = jnp.maximum(down, 0)
    lower = step * (half // step - 1 - lax.div(down, step)) + lax.rem(down, step)
    return jnp.where(place < half, place + half, lower)


def over_tokens(left, right):
    return lax.dot_general(left, right, (((0,), (0,)), ((), ())), preferred_element_type=jnp.float32)


def over_features(left, right):
    return lax.dot_general(left, right, (((1,), (1,)), ((), ())), preferred_element_type=jnp.float32)


def group_sums(values, width):
    lane = lax.broadcasted_iota(jnp.int32, values.shape, 1)
    step = 1
    while step < width:
        below = pltpu.roll(values, step, 1)
        above = pltpu.roll(values, LANES - step, 1)
        values = values + jnp.where((lane & step) != 0, below, above)
        step *= 2
    return values


def loss_parts(loss):
    whole = jnp.full((TAIL, LANES), loss, jnp.float32)
    high = whole.astype(jnp.bfloat16).astype(jnp.float32)
    middle = (whole - high).astype(jnp.bfloat16).astype(jnp.float32)
    low = whole - high - middle
    lane = lax.broadcasted_iota(jnp.int32, (TAIL, LANES), 1)
    parts = jnp.where(lane == 0, high, jnp.where(lane == 1, middle, jnp.where(lane == 2, low, 0.0)))
    return parts.astype(jnp.bfloat16)


def loss_of(parts):
    return jnp.sum(parts.astype(jnp.float32)[:1])


def ask_body(queries_ref, out_ref, sems):
    copies = [
        pltpu.make_async_copy(queries_ref, out_ref.at[k], sems.at[k]) for k in range(out_ref.shape[0])
    ]
    for copy in copies:
        copy.start()
    for copy in copies:
        copy.wait()


class Page:
    def __init__(self, query_len, page_len, query_rows, near, far, bias_near, bias_far, sign):
        _, width = near.shape
        block_rows = query_rows.shape[0]
        pieces = block_rows // LANES
        scale = width ** (-0.5)
        rate = scale * math.log2(math.e)
        gain = LOGIT_SPAN / query_len
        centre = query_len * (CENTRE_SHIFT + math.log(FILL_SHARE * page_len))
        lane = lax.broadcasted_iota(jnp.int32, (block_rows, LANES), 1)
        one = jnp.where(lane == 0, 1.0, 0.0).astype(jnp.bfloat16)
        wide_rows = jnp.concatenate([query_rows, one], axis=1)
        raw_near = over_features(jnp.concatenate([near, bias_near], axis=1), wide_rows)
        raw_far = over_features(jnp.concatenate([far, bias_far], axis=1), wide_rows)
        highest = jnp.maximum(
            jnp.max(raw_near, axis=0, keepdims=True), jnp.max(raw_far, axis=0, keepdims=True)
        )
        self.exp_near = jnp.exp2((raw_near - highest) * rate)
        self.exp_far = jnp.exp2((raw_far - highest) * rate)
        total = jnp.sum(self.exp_near, axis=0, keepdims=True) + jnp.sum(self.exp_far, axis=0, keepdims=True)

        def stacked(v):
            return jnp.concatenate([v[:, LANES * k : LANES * (k + 1)] for k in range(pieces)], axis=0)

        sums = stacked(total)
        smooth = stacked(highest) * scale + jnp.log(sums)
        similarity = group_sums(smooth, query_len)
        sign = stacked(sign)
        against = -sign * (gain * (similarity - centre))
        small = jnp.exp(-jnp.abs(against))
        losses = jnp.maximum(against, 0.0) + jnp.log1p(small)
        sigmoid = jnp.where(against >= 0.0, 1.0, small) / (1.0 + small)
        factor = (-gain * sign) * sigmoid / sums
        self.factor = jnp.concatenate([factor[k : k + 1, :] for k in range(pieces)], axis=1)
        lane = lax.broadcasted_iota(jnp.int32, losses.shape, 1)
        self.loss = jnp.sum(jnp.where(lane % query_len == 0, losses, 0.0))

    def near(self):
        return (self.exp_near * self.factor).astype(jnp.bfloat16)

    def query_terms(self, near, far):
        terms = over_tokens(near, self.exp_near.astype(jnp.bfloat16))
        return (terms + over_tokens(far, self.exp_far.astype(jnp.bfloat16))) * self.factor


def in_blocks(row_count, body):
    block_rows = math.gcd(row_count, ROW_BLOCK)
    count = row_count // block_rows
    if count == 1:
        body(0, block_rows, True)
        return

    @pl.loop(0, count)
    def _(index):
        body(index, block_rows, index == 0)


def add_to(ref, value, first):
    if first is True:
        ref[...] = value
    else:
        ref[...] = jnp.where(first, 0.0, ref[...]) + value


def step_body(
    query_len, page_len, bias_ref, rows_ref, near_ref, far_ref, near2_ref, far2_ref, sign_ref,
    blocks_ref, sums_ref, loss_ref, held, kept, factors, sem,
):
    row_count, width = rows_ref.shape
    copies, dest_rows = held.shape[1:3]
    out = pltpu.make_async_copy(held, blocks_ref, sem)

    def body(index, block_rows, first):
        offset = pl.multiple_of(index * block_rows, block_rows)
        query_rows = rows_ref[pl.ds(offset, block_rows), :]
        near, far, near2, far2 = near_ref[...], far_ref[...], near2_ref[...], far2_ref[...]
        one, two = (
            Page(
                query_len, page_len, query_rows, a, b, bias_ref[2 * k], bias_ref[2 * k + 1],
                sign_ref[0, k : k + 1, pl.ds(offset, block_rows)],
            )
            for k, (a, b) in enumerate(((near, far), (near2, far2)))
        )
        terms = one.query_terms(near, far) + two.query_terms(near2, far2)
        dests = block_rows // dest_rows
        shaped = terms.T.astype(jnp.bfloat16).reshape(dests, dest_rows, width)
        for d in range(dests):
            chips = held.shape[0]
            place = (chip_at(index * dests + d, chips) + chips - chips // 2 - SHIFT) % chips
            for k in range(copies):
                held[place, k] = shaped[d]
        for k, page in enumerate((one, two)):
            kept[k] = page.exp_near
            factors[k] = page.factor
        if first is True:
            out.start()
        row = lax.broadcasted_iota(jnp.int32, loss_ref.shape, 0)
        add_to(loss_ref, jnp.where(row == 0, one.loss, two.loss), first)

        @pl.loop(0, 2)
        def _(page):
            scaled = (kept[page] * factors[page]).astype(jnp.bfloat16)
            add_to(
                sums_ref.at[page],
                jnp.dot(scaled, rows_ref[pl.ds(offset, block_rows), :], preferred_element_type=jnp.float32),
                first,
            )

    in_blocks(row_count, body)
    if row_count != math.gcd(row_count, ROW_BLOCK):
        out.start()
    out.wait()


def rest_body(
    query_len, page_len, bias_ref, rows_ref, near_ref, far_ref, near2_ref, far2_ref, sign_ref,
    sums_ref, loss_in, near_out, sent_ref, loss_out, near_sum, near2_sum, loss_sum,
):
    row_count, width = rows_ref.shape
    tokens = near_ref.shape[0]
    scale = width ** (-0.5)

    def body(index, block_rows, first):
        offset = pl.multiple_of(index * block_rows, block_rows)
        query_rows = rows_ref[pl.ds(offset, block_rows), :]
        one, two = (
            Page(
                query_len, page_len, query_rows, a[...], b[...], bias_ref[2 * k], bias_ref[2 * k + 1],
                sign_ref[1, k : k + 1, pl.ds(offset, block_rows)],
            )
            for k, (a, b) in enumerate(((near_ref, far_ref), (near2_ref, far2_ref)))
        )
        add_to(near_sum, jnp.dot(one.near(), query_rows, preferred_element_type=jnp.float32), first)
        add_to(near2_sum, jnp.dot(two.near(), query_rows, preferred_element_type=jnp.float32), first)
        row = lax.broadcasted_iota(jnp.int32, loss_sum.shape, 0)
        add_to(loss_sum, jnp.where(row == 0, one.loss, two.loss), first)

    in_blocks(row_count, body)
    near_out[...] = (near_sum[...] + sums_ref[0]) * scale
    sent_ref[pl.ds(0, tokens), :] = ((near2_sum[...] + sums_ref[1]) * scale).astype(jnp.bfloat16)
    losses = loss_in[...] + loss_sum[...]
    loss_out[...] = losses
    sent_ref[pl.ds(tokens, TAIL), :] = loss_parts(jnp.max(losses[1:2]))


def bias_body(query_count, query_len, facts_ref, facts2_ref, bias_ref, sign_ref):
    tokens = bias_ref.shape[1]
    shares, _, row_count = sign_ref.shape
    share = lax.axis_index("tok")
    side = lax.rem(lax.axis_index("pages"), 2)
    picked = query_count // shares
    chips = row_count // (picked * query_len)
    row = lax.broadcasted_iota(jnp.int32, bias_ref.shape[1:], 0)
    lane = lax.broadcasted_iota(jnp.int32, bias_ref.shape[1:], 1)
    group = lax.broadcasted_iota(jnp.int32, (1, LANES), 1) // query_len
    for page, ref in enumerate((facts_ref, facts2_ref)):
        usable = shares * tokens - ref[ref.shape[0] - 1]
        for half in range(shares):
            first = lax.rem(share + half, shares) * tokens
            padding = (row >= usable - first) & (lane == 0)
            bias_ref[shares * page + half] = jnp.where(padding, MASKED, 0.0).astype(jnp.bfloat16)
        for slot in range(shares):
            start = lax.rem(share + slot, shares) * picked
            for piece in range(row_count // LANES):
                signs = jnp.zeros((1, LANES), jnp.float32)
                for k in range(LANES // query_len):
                    place = piece * (LANES // query_len) + k
                    chip = chip_at(place // picked, chips)
                    label = ref[(2 * chip + side) * query_count + start + place % picked]
                    signs = jnp.where(group == k, 2.0 * label.astype(jnp.float32) - 1.0, signs)
                sign_ref[slot, page : page + 1, pl.ds(piece * LANES, LANES)] = signs


def last_body(near_ref, loss_ref, got_ref, grad_ref, total_ref):
    tokens = near_ref.shape[0]
    grad_ref[0] = near_ref[...] + got_ref[pl.ds(0, tokens), :].astype(jnp.float32)
    total_ref[0] = jnp.max(loss_ref[0:1, :]) + loss_of(got_ref[pl.ds(tokens, TAIL), :])


def device_step(queries, pages, pad_counts, labels):
    query_count, query_len, width = queries.shape
    _, tokens, _ = pages.shape
    owners = lax.axis_size("pages")
    shares = lax.axis_size("tok")
    if shares != 2 or query_count % shares or owners % 2:
        raise ValueError("unsupported split")
    share = lax.axis_index("tok")
    page_len = tokens * shares
    picked = query_count // shares
    dest_rows = picked * query_len
    chips = owners // 2
    swap = [(0, 1), (1, 0)]
    partner = [(i, i ^ 1) for i in range(owners)]
    order = [chip_at(j, chips) for j in range(chips)]
    same_side = [[2 * j + c for j in order] for c in range(2)]
    later = [(j + chips // 2 + SHIFT) % chips for j in range(chips)]
    same_side_all = [
        [(2 * j + c) * shares + k for j in later for k in range(shares)] for c in range(2)
    ]
    vmem = pl.BlockSpec(memory_space=pltpu.VMEM)
    smem = pl.BlockSpec(memory_space=pltpu.SMEM)
    anywhere = pl.BlockSpec(memory_space=pl.ANY)
    params = pltpu.CompilerParams(vmem_limit_bytes=VMEM_BYTES)

    asked = pl.pallas_call(
        ask_body,
        out_shape=jax.ShapeDtypeStruct((chips, query_count, query_len, width), queries.dtype),
        in_specs=[anywhere],
        out_specs=anywhere,
        scratch_shapes=[pltpu.SemaphoreType.DMA((chips,))],
        compiler_params=params,
        name="ask_copies",
    )(queries)
    gathered = lax.all_to_all(
        asked.reshape(chips, query_count * query_len, width),
        "pages", 0, 0, tiled=True, axis_index_groups=same_side,
    ).reshape(chips, shares, dest_rows, width)

    near = pages[0]
    far = lax.ppermute(near, "tok", swap)
    near2 = lax.ppermute(near, "pages", partner)
    far2 = lax.ppermute(far, "pages", partner)
    facts = jnp.concatenate([labels[:, 0], pad_counts])
    facts2 = lax.ppermute(facts, "pages", partner)

    def of_share(index):
        return lax.dynamic_index_in_dim(gathered, index, 1, False).reshape(row_count, width)

    row_count = chips * dest_rows
    rows = of_share(share)
    rows_b = of_share(1 - share)
    half = jax.ShapeDtypeStruct((tokens, width), jnp.float32)
    lane_row = jax.ShapeDtypeStruct((8, LANES), jnp.float32)
    bias, signs = pl.pallas_call(
        functools.partial(bias_body, query_count, query_len),
        out_shape=(
            jax.ShapeDtypeStruct((2 * shares, tokens, LANES), jnp.bfloat16),
            jax.ShapeDtypeStruct((shares, 2, row_count), jnp.float32),
        ),
        in_specs=[smem, smem],
        out_specs=(vmem, vmem),
        cost_estimate=pl.CostEstimate(flops=0, transcendentals=0, bytes_accessed=8 * tokens * width),
        compiler_params=params,
        name="page_bias",
    )(facts, facts2)
    block_rows = math.gcd(row_count, ROW_BLOCK)
    blocks, sums, loss = pl.pallas_call(
        functools.partial(step_body, query_len, page_len),
        out_shape=(
            jax.ShapeDtypeStruct((chips, shares, dest_rows, width), jnp.bfloat16),
            jax.ShapeDtypeStruct((2, tokens, width), jnp.float32),
            lane_row,
        ),
        in_specs=[vmem] * 7,
        out_specs=(anywhere, vmem, vmem),
        scratch_shapes=[
            pltpu.VMEM((chips, shares, dest_rows, width), jnp.bfloat16),
            pltpu.VMEM((2, tokens, block_rows), jnp.float32),
            pltpu.VMEM((2, 1, block_rows), jnp.float32),
            pltpu.SemaphoreType.DMA,
        ],
        cost_estimate=pl.CostEstimate(
            flops=10 * row_count * page_len * width,
            transcendentals=2 * row_count * page_len,
            bytes_accessed=6 * row_count * width + 20 * tokens * width,
        ),
        compiler_params=params,
        name="page_step",
    )(bias, rows, near, far, near2, far2, signs)

    partials = lax.all_to_all(
        blocks.reshape(chips * shares, dest_rows, width),
        ("pages", "tok"), 0, 0, tiled=True, axis_index_groups=same_side_all,
    )
    near_sum, sent, loss = pl.pallas_call(
        functools.partial(rest_body, query_len, page_len),
        out_shape=(half, jax.ShapeDtypeStruct((tokens + TAIL, width), jnp.bfloat16), lane_row),
        in_specs=[vmem] * 9,
        out_specs=(vmem,) * 3,
        scratch_shapes=[pltpu.VMEM((tokens, width), jnp.float32)] * 2 + [pltpu.VMEM((8, LANES), jnp.float32)],
        cost_estimate=pl.CostEstimate(
            flops=6 * row_count * page_len * width,
            transcendentals=2 * row_count * page_len,
            bytes_accessed=2 * row_count * width + 20 * tokens * width,
        ),
        compiler_params=params,
        name="page_rest",
    )(bias, rows_b, near, far, near2, far2, signs, sums, loss)
    got = lax.ppermute(sent, "pages", partner)
    page_grad, page_loss = pl.pallas_call(
        last_body,
        out_shape=(
            jax.ShapeDtypeStruct((1, tokens, width), jnp.float32),
            jax.ShapeDtypeStruct((1,), jnp.float32),
        ),
        in_specs=[vmem, vmem, vmem],
        out_specs=(vmem, smem),
        cost_estimate=pl.CostEstimate(flops=2 * tokens * width, transcendentals=0, bytes_accessed=12 * tokens * width),
        compiler_params=params,
        name="page_out",
    )(near_sum, loss, got)
    summed = jnp.sum(
        partials.reshape(chips, shares, dest_rows, width).astype(jnp.float32), axis=0
    ) * (width ** (-0.5))
    query_grad = summed.reshape(query_count, query_len, width)
    return query_grad, page_grad, page_loss


def solution(mesh):
    return jax.shard_map(
        device_step,
        mesh=mesh,
        in_specs=(P("pages", None, None), P("pages", "tok", None), P("pages"), P(None, "pages")),
        out_specs=(P("pages", None, None), P("pages", "tok", None), P("pages")),
        check_vma=False,
    )
```

```python
import functools
import math

import jax
import jax.numpy as jnp
from jax import lax
from jax.experimental import pallas as pl
from jax.experimental.pallas import tpu as pltpu
from jax.sharding import PartitionSpec as P


MASKED = -1.0e30
LOGIT_SPAN = 8.0
CENTRE_SHIFT = 0.5
FILL_SHARE = 0.75
LANES = 128
ROW_BLOCK = 256
TAIL = 16
SHIFT = 1
VMEM_BYTES = 24 * 2**20


def chip_at(place, chips):
    half = chips // 2
    step = 1 if half % 2 else 2
    down = place - half
    if isinstance(place, int):
        return place + half if down < 0 else step * (half // step - 1 - down // step) + down % step
    down = jnp.maximum(down, 0)
    lower = step * (half // step - 1 - lax.div(down, step)) + lax.rem(down, step)
    return jnp.where(place < half, place + half, lower)


def over_tokens(left, right):
    return lax.dot_general(left, right, (((0,), (0,)), ((), ())), preferred_element_type=jnp.float32)


def over_features(left, right):
    return lax.dot_general(left, right, (((1,), (1,)), ((), ())), preferred_element_type=jnp.float32)


def group_sums(values, width):
    lane = lax.broadcasted_iota(jnp.int32, values.shape, 1)
    step = 1
    while step < width:
        below = pltpu.roll(values, step, 1)
        above = pltpu.roll(values, LANES - step, 1)
        values = values + jnp.where((lane & step) != 0, below, above)
        step *= 2
    return values


def loss_parts(loss):
    whole = jnp.full((TAIL, LANES), loss, jnp.float32)
    high = whole.astype(jnp.bfloat16).astype(jnp.float32)
    middle = (whole - high).astype(jnp.bfloat16).astype(jnp.float32)
    low = whole - high - middle
    lane = lax.broadcasted_iota(jnp.int32, (TAIL, LANES), 1)
    parts = jnp.where(lane == 0, high, jnp.where(lane == 1, middle, jnp.where(lane == 2, low, 0.0)))
    return parts.astype(jnp.bfloat16)


def loss_of(parts):
    return jnp.sum(parts.astype(jnp.float32)[:1])


def ask_body(queries_ref, out_ref, sems):
    copies = [
        pltpu.make_async_copy(queries_ref, out_ref.at[k], sems.at[k]) for k in range(out_ref.shape[0])
    ]
    for copy in copies:
        copy.start()
    for copy in copies:
        copy.wait()


class Page:
    def __init__(self, query_len, page_len, query_rows, near, far, bias_near, bias_far, sign):
        _, width = near.shape
        block_rows = query_rows.shape[0]
        pieces = block_rows // LANES
        scale = width ** (-0.5)
        rate = scale * math.log2(math.e)
        gain = LOGIT_SPAN / query_len
        centre = query_len * (CENTRE_SHIFT + math.log(FILL_SHARE * page_len))
        lane = lax.broadcasted_iota(jnp.int32, (block_rows, LANES), 1)
        one = jnp.where(lane == 0, 1.0, 0.0).astype(jnp.bfloat16)
        wide_rows = jnp.concatenate([query_rows, one], axis=1)
        raw_near = over_features(jnp.concatenate([near, bias_near], axis=1), wide_rows)
        raw_far = over_features(jnp.concatenate([far, bias_far], axis=1), wide_rows)
        highest = jnp.maximum(
            jnp.max(raw_near, axis=0, keepdims=True), jnp.max(raw_far, axis=0, keepdims=True)
        )
        self.exp_near = jnp.exp2((raw_near - highest) * rate)
        self.exp_far = jnp.exp2((raw_far - highest) * rate)
        total = jnp.sum(self.exp_near, axis=0, keepdims=True) + jnp.sum(self.exp_far, axis=0, keepdims=True)

        def stacked(v):
            return jnp.concatenate([v[:, LANES * k : LANES * (k + 1)] for k in range(pieces)], axis=0)

        sums = stacked(total)
        smooth = stacked(highest) * scale + jnp.log(sums)
        similarity = group_sums(smooth, query_len)
        sign = stacked(sign)
        against = -sign * (gain * (similarity - centre))
        small = jnp.exp(-jnp.abs(against))
        losses = jnp.maximum(against, 0.0) + jnp.log1p(small)
        sigmoid = jnp.where(against >= 0.0, 1.0, small) / (1.0 + small)
        factor = (-gain * sign) * sigmoid / sums
        self.factor = jnp.concatenate([factor[k : k + 1, :] for k in range(pieces)], axis=1)
        lane = lax.broadcasted_iota(jnp.int32, losses.shape, 1)
        self.loss = jnp.sum(jnp.where(lane % query_len == 0, losses, 0.0))

    def near(self):
        return (self.exp_near * self.factor).astype(jnp.bfloat16)

    def query_terms(self, near, far):
        terms = over_tokens(near, self.exp_near.astype(jnp.bfloat16))
        return (terms + over_tokens(far, self.exp_far.astype(jnp.bfloat16))) * self.factor


def in_blocks(row_count, body):
    block_rows = math.gcd(row_count, ROW_BLOCK)
    count = row_count // block_rows
    if count == 1:
        body(0, block_rows, True)
        return

    @pl.loop(0, count)
    def _(index):
        body(index, block_rows, index == 0)


def add_to(ref, value, first):
    if first is True:
        ref[...] = value
    else:
        ref[...] = jnp.where(first, 0.0, ref[...]) + value


def step_body(
    query_len, page_len, bias_ref, rows_ref, near_ref, far_ref, near2_ref, far2_ref, sign_ref,
    blocks_ref, sums_ref, loss_ref, held, kept, factors, sem,
):
    row_count, width = rows_ref.shape
    copies, dest_rows = held.shape[1:3]
    out = pltpu.make_async_copy(held, blocks_ref, sem)

    def body(index, block_rows, first):
        offset = pl.multiple_of(index * block_rows, block_rows)
        query_rows = rows_ref[pl.ds(offset, block_rows), :]
        near, far, near2, far2 = near_ref[...], far_ref[...], near2_ref[...], far2_ref[...]
        one, two = (
            Page(
                query_len, page_len, query_rows, a, b, bias_ref[2 * k], bias_ref[2 * k + 1],
                sign_ref[0, k : k + 1, pl.ds(offset, block_rows)],
            )
            for k, (a, b) in enumerate(((near, far), (near2, far2)))
        )
        terms = one.query_terms(near, far) + two.query_terms(near2, far2)
        dests = block_rows // dest_rows
        shaped = terms.T.astype(jnp.bfloat16).reshape(dests, dest_rows, width)
        for d in range(dests):
            chips = held.shape[0]
            place = (chip_at(index * dests + d, chips) + chips - chips // 2 - SHIFT) % chips
            for k in range(copies):
                held[place, k] = shaped[d]
        for k, page in enumerate((one, two)):
            kept[k] = page.exp_near
            factors[k] = page.factor
        if first is True:
            out.start()
        row = lax.broadcasted_iota(jnp.int32, loss_ref.shape, 0)
        add_to(loss_ref, jnp.where(row == 0, one.loss, two.loss), first)

        @pl.loop(0, 2)
        def _(page):
            scaled = (kept[page] * factors[page]).astype(jnp.bfloat16)
            add_to(
                sums_ref.at[page],
                jnp.dot(scaled, rows_ref[pl.ds(offset, block_rows), :], preferred_element_type=jnp.float32),
                first,
            )

    in_blocks(row_count, body)
    if row_count != math.gcd(row_count, ROW_BLOCK):
        out.start()
    out.wait()


def rest_body(
    query_len, page_len, bias_ref, rows_ref, near_ref, far_ref, near2_ref, far2_ref, sign_ref,
    sums_ref, loss_in, near_out, sent_ref, loss_out, near_sum, near2_sum, loss_sum,
):
    row_count, width = rows_ref.shape
    tokens = near_ref.shape[0]
    scale = width ** (-0.5)

    def body(index, block_rows, first):
        offset = pl.multiple_of(index * block_rows, block_rows)
        query_rows = rows_ref[pl.ds(offset, block_rows), :]
        one, two = (
            Page(
                query_len, page_len, query_rows, a[...], b[...], bias_ref[2 * k], bias_ref[2 * k + 1],
                sign_ref[1, k : k + 1, pl.ds(offset, block_rows)],
            )
            for k, (a, b) in enumerate(((near_ref, far_ref), (near2_ref, far2_ref)))
        )
        add_to(near_sum, jnp.dot(one.near(), query_rows, preferred_element_type=jnp.float32), first)
        add_to(near2_sum, jnp.dot(two.near(), query_rows, preferred_element_type=jnp.float32), first)
        row = lax.broadcasted_iota(jnp.int32, loss_sum.shape, 0)
        add_to(loss_sum, jnp.where(row == 0, one.loss, two.loss), first)

    in_blocks(row_count, body)
    near_out[...] = (near_sum[...] + sums_ref[0]) * scale
    sent_ref[pl.ds(0, tokens), :] = ((near2_sum[...] + sums_ref[1]) * scale).astype(jnp.bfloat16)
    losses = loss_in[...] + loss_sum[...]
    loss_out[...] = losses
    sent_ref[pl.ds(tokens, TAIL), :] = loss_parts(jnp.max(losses[1:2]))


def bias_body(query_count, query_len, facts_ref, facts2_ref, bias_ref, sign_ref):
    tokens = bias_ref.shape[1]
    shares, _, row_count = sign_ref.shape
    share = lax.axis_index("tok")
    side = lax.rem(lax.axis_index("pages"), 2)
    picked = query_count // shares
    chips = row_count // (picked * query_len)
    row = lax.broadcasted_iota(jnp.int32, bias_ref.shape[1:], 0)
    lane = lax.broadcasted_iota(jnp.int32, bias_ref.shape[1:], 1)
    group = lax.broadcasted_iota(jnp.int32, (1, LANES), 1) // query_len
    for page, ref in enumerate((facts_ref, facts2_ref)):
        usable = shares * tokens - ref[ref.shape[0] - 1]
        for half in range(shares):
            first = lax.rem(share + half, shares) * tokens
            padding = (row >= usable - first) & (lane == 0)
            bias_ref[shares * page + half] = jnp.where(padding, MASKED, 0.0).astype(jnp.bfloat16)
        for slot in range(shares):
            start = lax.rem(share + slot, shares) * picked
            for piece in range(row_count // LANES):
                signs = jnp.zeros((1, LANES), jnp.float32)
                for k in range(LANES // query_len):
                    place = piece * (LANES // query_len) + k
                    chip = chip_at(place // picked, chips)
                    label = ref[(2 * chip + side) * query_count + start + place % picked]
                    signs = jnp.where(group == k, 2.0 * label.astype(jnp.float32) - 1.0, signs)
                sign_ref[slot, page : page + 1, pl.ds(piece * LANES, LANES)] = signs


def last_body(near_ref, loss_ref, got_ref, grad_ref, total_ref):
    tokens = near_ref.shape[0]
    grad_ref[0] = near_ref[...] + got_ref[pl.ds(0, tokens), :].astype(jnp.float32)
    total_ref[0] = jnp.max(loss_ref[0:1, :]) + loss_of(got_ref[pl.ds(tokens, TAIL), :])


def device_step(queries, pages, pad_counts, labels):
    query_count, query_len, width = queries.shape
    _, tokens, _ = pages.shape
    owners = lax.axis_size("pages")
    shares = lax.axis_size("tok")
    if shares != 2 or query_count % shares or owners % 2:
        raise ValueError("unsupported split")
    share = lax.axis_index("tok")
    page_len = tokens * shares
    picked = query_count // shares
    dest_rows = picked * query_len
    chips = owners // 2
    swap = [(0, 1), (1, 0)]
    partner = [(i, i ^ 1) for i in range(owners)]
    order = [chip_at(j, chips) for j in range(chips)]
    same_side = [[2 * j + c for j in order] for c in range(2)]
    later = [(j + chips // 2 + SHIFT) % chips for j in range(chips)]
    same_side_all = [
        [(2 * j + c) * shares + k for j in later for k in range(shares)] for c in range(2)
    ]
    vmem = pl.BlockSpec(memory_space=pltpu.VMEM)
    smem = pl.BlockSpec(memory_space=pltpu.SMEM)
    anywhere = pl.BlockSpec(memory_space=pl.ANY)
    params = pltpu.CompilerParams(vmem_limit_bytes=VMEM_BYTES)
    packed = pltpu.CompilerParams(vmem_limit_bytes=VMEM_BYTES)

    asked = pl.pallas_call(
        ask_body,
        out_shape=jax.ShapeDtypeStruct((chips, query_count, query_len, width), queries.dtype),
        in_specs=[anywhere],
        out_specs=anywhere,
        scratch_shapes=[pltpu.SemaphoreType.DMA((chips,))],
        compiler_params=params,
        name="ask_copies",
    )(queries)
    gathered = lax.all_to_all(
        asked.reshape(chips, query_count * query_len, width),
        "pages", 0, 0, tiled=True, axis_index_groups=same_side,
    ).reshape(chips, shares, dest_rows, width)

    near = pages[0]
    far = lax.ppermute(near, "tok", swap)
    near2 = lax.ppermute(near, "pages", partner)
    far2 = lax.ppermute(far, "pages", partner)
    facts = jnp.concatenate([labels[:, 0], pad_counts])
    facts2 = lax.ppermute(facts, "pages", partner)

    def of_share(index):
        return lax.dynamic_index_in_dim(gathered, index, 1, False).reshape(row_count, width)

    row_count = chips * dest_rows
    rows = of_share(share)
    rows_b = of_share(1 - share)
    half = jax.ShapeDtypeStruct((tokens, width), jnp.float32)
    lane_row = jax.ShapeDtypeStruct((8, LANES), jnp.float32)
    bias, signs = pl.pallas_call(
        functools.partial(bias_body, query_count, query_len),
        out_shape=(
            jax.ShapeDtypeStruct((2 * shares, tokens, LANES), jnp.bfloat16),
            jax.ShapeDtypeStruct((shares, 2, row_count), jnp.float32),
        ),
        in_specs=[smem, smem],
        out_specs=(vmem, vmem),
        cost_estimate=pl.CostEstimate(flops=0, transcendentals=0, bytes_accessed=8 * tokens * width),
        compiler_params=params,
        name="page_bias",
    )(facts, facts2)
    block_rows = math.gcd(row_count, ROW_BLOCK)
    blocks, sums, loss = pl.pallas_call(
        functools.partial(step_body, query_len, page_len),
        out_shape=(
            jax.ShapeDtypeStruct((chips, shares, dest_rows, width), jnp.bfloat16),
            jax.ShapeDtypeStruct((2, tokens, width), jnp.float32),
            lane_row,
        ),
        in_specs=[vmem] * 7,
        out_specs=(anywhere, vmem, vmem),
        scratch_shapes=[
            pltpu.VMEM((chips, shares, dest_rows, width), jnp.bfloat16),
            pltpu.VMEM((2, tokens, block_rows), jnp.float32),
            pltpu.VMEM((2, 1, block_rows), jnp.float32),
            pltpu.SemaphoreType.DMA,
        ],
        cost_estimate=pl.CostEstimate(
            flops=10 * row_count * page_len * width,
            transcendentals=2 * row_count * page_len,
            bytes_accessed=6 * row_count * width + 20 * tokens * width,
        ),
        compiler_params=packed,
        name="page_step",
    )(bias, rows, near, far, near2, far2, signs)

    partials = lax.all_to_all(
        blocks.reshape(chips * shares, dest_rows, width),
        ("pages", "tok"), 0, 0, tiled=True, axis_index_groups=same_side_all,
    )
    near_sum, sent, loss = pl.pallas_call(
        functools.partial(rest_body, query_len, page_len),
        out_shape=(half, jax.ShapeDtypeStruct((tokens + TAIL, width), jnp.bfloat16), lane_row),
        in_specs=[vmem] * 9,
        out_specs=(vmem,) * 3,
        scratch_shapes=[pltpu.VMEM((tokens, width), jnp.float32)] * 2 + [pltpu.VMEM((8, LANES), jnp.float32)],
        cost_estimate=pl.CostEstimate(
            flops=6 * row_count * page_len * width,
            transcendentals=2 * row_count * page_len,
            bytes_accessed=2 * row_count * width + 20 * tokens * width,
        ),
        compiler_params=packed,
        name="page_rest",
    )(bias, rows_b, near, far, near2, far2, signs, sums, loss)
    got = lax.ppermute(sent, "pages", partner)
    page_grad, page_loss = pl.pallas_call(
        last_body,
        out_shape=(
            jax.ShapeDtypeStruct((1, tokens, width), jnp.float32),
            jax.ShapeDtypeStruct((1,), jnp.float32),
        ),
        in_specs=[vmem, vmem, vmem],
        out_specs=(vmem, smem),
        cost_estimate=pl.CostEstimate(flops=2 * tokens * width, transcendentals=0, bytes_accessed=12 * tokens * width),
        compiler_params=params,
        name="page_out",
    )(near_sum, loss, got)
    summed = jnp.sum(
        partials.reshape(chips, shares, dest_rows, width).astype(jnp.float32), axis=0
    ) * (width ** (-0.5))
    query_grad = summed.reshape(query_count, query_len, width)
    return query_grad, page_grad, page_loss


def solution(mesh):
    return jax.shard_map(
        device_step,
        mesh=mesh,
        in_specs=(P("pages", None, None), P("pages", "tok", None), P("pages"), P(None, "pages")),
        out_specs=(P("pages", None, None), P("pages", "tok", None), P("pages")),
        check_vma=False,
    )
```
